32 devices in a mesh: gx: 2 (over core), gy: 4 (over y, x), gz: 4 (over z).
Axes of the slice: x: 2, y: 2, z: 4, core: 2. Of those that a mesh axis runs over, the one named last changes fastest.
Arguments:
- offsets: float32 [3, 4, 8, 8, 128], P(None, 'gx', 'gy', 'gz'), may hold values from 0 to 1
- velocity: float32 [3, 4, 8, 8, 128], P(None, 'gx', 'gy', 'gz'), may hold values from -6 to 6
- mass: float32 [4, 8, 8, 128], P('gx', 'gy', 'gz'), may hold values from 0.005 to 0.02
- counts: int32 [4, 8, 8], P('gx', 'gy', 'gz'), may hold values from 1 to 128
Outputs:
- accel: float32 [3, 4, 8, 8, 128], P(None, 'gx', 'gy', 'gz')
- density: float32 [4, 8, 8, 128], P('gx', 'gy', 'gz')
The draws below stay inside these ranges and needn't reach their ends.
Inputs may be any that keep to these rules, and one draw needn't show every extreme that they name: `counts`: slots of a cell at or beyond its count are empty.
All inputs are finite; a program needn't handle non-finite values.
Results may differ from the reference program's by a relative error of at most 0.0003.
Values sent between devices are 32-bit elements; how exact they have to be, the bound alone decides.
No kernel may reach another device: no remote copies, remote signals or barrier semaphores. Data moves between devices by JAX's collectives and lax.ppermute only.
A program may use at most 64 MiB of HBM per device.

```python
import math
import jax
import jax.numpy as jnp
from jax import lax

P_SIZE = 128
NCX = 4
NCY = 8
NCZ = 8


def touch_ends(values, own_key, low, high):
    extent = values.shape
    place = [jax.random.randint(jax.random.fold_in(own_key, axis), (), 0, extent[axis]) for axis in range(len(extent))]
    values = values.at[tuple(place)].set(low)
    longest = extent.index(max(extent))
    place[longest] = (place[longest] + 1) % extent[longest]
    return values.at[tuple(place)].set(high)


def block_scale(own_key, extent, pieces, least, top_value):
    def one(dim, parts):
        heights = jax.random.uniform(jax.random.fold_in(jax.random.fold_in(own_key, 6), dim), (parts,), jnp.float32, least / len(pieces), top_value / len(pieces))
        return jnp.repeat(jnp.exp(heights), extent[dim] // parts).reshape((-1,) + (1,) * (len(extent) - dim - 1))

    factor_of = one(*pieces[0])
    for cut in pieces[1:]:
        factor_of = factor_of * one(*cut)
    return factor_of


def normal_values(key, extent, spread, most, split=(), held_as=jnp.bfloat16):
    gain = block_scale(key, extent, split, -0.22, 0.18) if split else 1.0
    values = jax.random.normal(key, extent, jnp.float32) * spread * gain
    return jnp.minimum(jnp.maximum(values, -most), most).astype(held_as)


def setup_inputs(seed: int = 0) -> dict:
    splits = jax.random.split(jax.random.key(seed), 5)
    offsets = jnp.clip(1.0 * jax.random.uniform(splits[0], (3, NCX, NCY, NCZ, P_SIZE), jnp.float32) ** block_scale(splits[0], (3, NCX, NCY, NCZ, P_SIZE), ((1, 2), (2, 4), (3, 4)), -0.2, 0.2), 0.0, 1.0)
    velocity = normal_values(splits[1], (3, NCX, NCY, NCZ, P_SIZE), 1.0, 6.0, ((1, 2), (2, 4), (3, 4)), jnp.float32)
    mass = jnp.clip(jnp.exp(math.log(0.02) - 1.3862944 * jax.random.uniform(splits[2], (NCX, NCY, NCZ, P_SIZE), jnp.float32) ** block_scale(splits[2], (NCX, NCY, NCZ, P_SIZE), ((0, 2), (1, 4), (2, 4)), -0.2, 0.2)), 0.005, 0.02)
    counts = touch_ends(jax.random.randint(splits[3], (NCX, NCY, NCZ), 1, P_SIZE + 1), jax.random.fold_in(splits[3], 1), 1, P_SIZE).astype(jnp.int32)
    return {"offsets": offsets, "velocity": velocity, "mass": mass, "counts": counts}


KERNEL_NORM = 315.0 / (64.0 * math.pi)
GRADIENT_NORM = 6.0 * KERNEL_NORM
PRESSURE_COEF = 0.5
VISCOSITY = 0.5
NEIGHBOUR_STEPS = [(a - 1, b - 1, c - 1) for a in range(3) for b in range(3) for c in range(3)]


def plane_map(plane_fn, own_cells, near_cells):
    planes = (jnp.moveaxis(own_cells, 1, 0), jnp.moveaxis(near_cells, 1, 0))
    results = lax.map(lambda items: plane_fn(items[0], items[1]), planes)
    return jnp.moveaxis(results, 0, 1)


def pair_geometry(own_pos, near_pos, offset_vec):
    displace = own_pos[..., :, None] - near_pos[..., None, :] - offset_vec[:, None, None, None, None]
    dist_sq = jnp.sum(displace * displace, axis=0)
    falloff = jnp.maximum(1.0 - dist_sq, 0.0)
    return displace, falloff


def density_plane(own_cells, near_cells, offset_vec):
    displace, falloff = pair_geometry(own_cells[0:3], near_cells[0:3], offset_vec)
    kernel = KERNEL_NORM * falloff * falloff * falloff
    return jnp.sum(near_cells[3][..., None, :] * kernel, axis=-1)[None]


def force_plane(own_cells, near_cells, offset_vec):
    displace, falloff = pair_geometry(own_cells[0:3], near_cells[0:3], offset_vec)
    kernel = KERNEL_NORM * falloff * falloff * falloff
    gradient = GRADIENT_NORM * falloff * falloff
    near_mass = near_cells[3][..., None, :]
    near_rho = jnp.where(near_mass > 0.0, near_cells[7][..., None, :], 1.0)
    near_press = PRESSURE_COEF / near_rho
    pair_coef = near_mass * (own_cells[6][..., :, None] + near_press) * gradient
    viscous = VISCOSITY * near_mass / near_rho * kernel
    pressure_part = jnp.sum(pair_coef[None] * displace, axis=-1)
    velocity_gap = near_cells[4:7][..., None, :] - own_cells[3:6][..., :, None]
    return pressure_part + jnp.sum(viscous[None] * velocity_gap, axis=-1)


def cell_slice(padded, step_x, step_y, step_z, size_x, size_y, size_z):
    return padded[:, 1 + step_x:1 + step_x + size_x, 1 + step_y:1 + step_y + size_y, 1 + step_z:1 + step_z + size_z]


def accumulate(plane_fn, own_cells, padded):
    size_x, size_y, size_z = own_cells.shape[1], own_cells.shape[2], own_cells.shape[3]
    running = None
    for step_x, step_y, step_z in NEIGHBOUR_STEPS:
        offset_vec = jnp.array([step_x, step_y, step_z], jnp.float32)
        near_cells = cell_slice(padded, step_x, step_y, step_z, size_x, size_y, size_z)
        contribution = plane_map(lambda own, near: plane_fn(own, near, offset_vec), own_cells, near_cells)
        running = contribution if running is None else running + contribution
    return running


def pad_cycle(field):
    return jnp.pad(field, ((0, 0), (1, 1), (1, 1), (1, 1), (0, 0)))


def reference(offsets, velocity, mass, counts):
    slot_index = lax.broadcasted_iota(jnp.int32, counts.shape + (P_SIZE,), 3)
    occupied = (slot_index < counts[..., None]).astype(jnp.float32)
    mass_eff = mass * occupied
    rim_state = pad_cycle(jnp.concatenate([offsets, mass_eff[None]], axis=0))
    density_raw = accumulate(density_plane, offsets, rim_state)
    density = density_raw * occupied[None]
    flow_state = pad_cycle(jnp.concatenate([velocity, density], axis=0))
    near_state = jnp.concatenate([rim_state, flow_state], axis=0)
    rho_safe = jnp.where(occupied[None] > 0.0, density, 1.0)
    own_state = jnp.concatenate([offsets, velocity, PRESSURE_COEF / rho_safe], axis=0)
    accel = accumulate(force_plane, own_state, near_state) * occupied[None]
    return accel, density[0]
```

```python
import functools
import math

import jax
import jax.numpy as jnp
from jax import lax
from jax.experimental import pallas as pl
from jax.experimental.pallas import tpu as pltpu
from jax.sharding import PartitionSpec as P

KERNEL_NORM = 315.0 / (64.0 * math.pi)
PRESSURE_COEF = 0.5
VISCOSITY = 0.5
SUB = 8


def partner_pairs(sizes, axis, kind):
    n, nx = sizes[axis], sizes["gx"]
    pairs = []
    for i in range(n):
        j = (i ^ 1) if kind == "A" else ((i - 1) ^ 1) + 1
        if i == 0 and kind == "B" or j >= n or j < 0:
            j = i
        pairs.append(j)
    if axis == "gx":
        if kind == "B":
            pairs[0], pairs[n - 1] = n - 1, 0
        return "gx", [(i, j) for i, j in enumerate(pairs)]
    if all(i != j for i, j in enumerate(pairs)):
        return axis, list(enumerate(pairs))
    out = []
    for x in range(nx):
        for i, j in enumerate(pairs):
            to = (x, j)
            if i == j and nx % 2 == 0:
                to = (x ^ 1, j)
            out.append((x * n + i, to[0] * n + to[1]))
    return ("gx", axis), out


def swap(message, sizes, axis, kind):
    names, pairs = partner_pairs(sizes, axis, kind)
    return lax.ppermute(message, names, pairs)


def kinds_of(n):
    return ("A", "B") if n > 2 else ("A",) if n > 1 else ()


def extend(cells, sizes, axis, dim):
    size = cells.shape[dim]
    parts = [cells]
    for kind in kinds_of(sizes[axis]):
        at = size - 1 if kind == "A" else 0
        parts.append(swap(lax.slice_in_dim(cells, at, at + 1, axis=dim), sizes, axis, kind))
    return jnp.concatenate(parts, axis=dim)


def order_of(size, n):
    return list(range(1, size + 1)) + [{"A": size + 1, "B": 0}[k] for k in kinds_of(n)]


class Plan:
    def __init__(self, sizes, extents):
        self.lx, self.ly, self.lz = extents
        self.X = order_of(self.lx, sizes["gx"])
        self.Y = order_of(self.ly, sizes["gy"])
        self.Z = order_of(self.lz, sizes["gz"])
        self.cells = len(self.X) * len(self.Y)
        self.own = [
            (x, y, z)
            for x in range(1, self.lx + 1)
            for y in range(1, self.ly + 1)
            for z in range(1, self.lz + 1)
        ]

    def neighbours(self, cell):
        out = []
        for step in [(a, b, c) for a in (-1, 0, 1) for b in (-1, 0, 1) for c in (-1, 0, 1)]:
            x, y, z = (p + s for p, s in zip(cell, step))
            if x not in self.X or y not in self.Y or z not in self.Z:
                continue
            column = self.X.index(x) * len(self.Y) + self.Y.index(y)
            if z == self.lz + 1:
                out.append((1, column, step))
            elif z == 0:
                out.append((2, column, step))
            else:
                out.append((0, column * self.lz + z - 1, step))
        return out

    def own_index(self, cell):
        x, y, z = cell
        return ((x - 1) * len(self.Y) + y - 1) * self.lz + z - 1


def row(ref, index):
    return ref[pl.ds(index, SUB, stride=0), :]


def density_kernel(plan, info, counts, block, za, zb, density, columns, sums):
    slots = block.shape[-1]
    near = (block, za, zb)
    ncell = [ref.shape[0] // 4 for ref in near]
    sign = [info[0].astype(jnp.float32), info[1].astype(jnp.float32), info[2].astype(jnp.float32)]
    for o, cell in enumerate(plan.own):
        base = plan.own_index(cell)
        for f in range(3):
            line = block[pl.ds(f * ncell[0] + base, 1), :]
            columns[f, :, :] = jnp.broadcast_to(line, (slots, slots)).T
        sums[...] = jnp.zeros_like(sums)

        def chunk(i, carry, cell=cell):
            at = pl.ds(pl.multiple_of(i * SUB, SUB), SUB)
            shifted = []
            for f in range(3):
                x = columns[f, at, :]
                shifted.append({-1: x + sign[f], 0: x, 1: x - sign[f]})
            total = None
            for piece, index, step in plan.neighbours(cell):
                ref, n = near[piece], ncell[piece]
                d = [shifted[f][step[f]] - row(ref, f * n + index) for f in range(3)]
                q = jnp.maximum(1.0 - (d[0] * d[0] + d[1] * d[1] + d[2] * d[2]), 0.0)
                term = row(ref, 3 * n + index) * (q * q * q)
                total = term if total is None else total + term
            sums[at, :] = total
            return carry

        lax.fori_loop(0, pl.cdiv(counts[o], SUB), chunk, 0)
        density[pl.ds(o, 1), :] = jnp.sum(sums[...].T, axis=0, keepdims=True)


def force_kernel(plan, info, counts, block, za, zb, fblock, fza, fzb, press, accel, columns, sums):
    slots = block.shape[-1]
    near = (block, za, zb)
    flow = (fblock, fza, fzb)
    ncell = [ref.shape[0] // 4 for ref in near]
    sign = [info[0].astype(jnp.float32), info[1].astype(jnp.float32), info[2].astype(jnp.float32)]
    owns = len(plan.own)
    for o, cell in enumerate(plan.own):
        base = plan.own_index(cell)
        for f in range(3):
            columns[f, :, :] = jnp.broadcast_to(block[pl.ds(f * ncell[0] + base, 1), :], (slots, slots)).T
            columns[3 + f, :, :] = jnp.broadcast_to(fblock[pl.ds(f * ncell[0] + base, 1), :], (slots, slots)).T
        columns[6, :, :] = jnp.broadcast_to(press[pl.ds(o, 1), :], (slots, slots)).T
        sums[...] = jnp.zeros_like(sums)

        def chunk(i, carry, cell=cell):
            at = pl.ds(pl.multiple_of(i * SUB, SUB), SUB)
            shifted = []
            for f in range(3):
                x = columns[f, at, :]
                shifted.append({-1: x + sign[f], 0: x, 1: x - sign[f]})
            v = [columns[3 + f, at, :] for f in range(3)]
            s = columns[6, at, :]
            total = [None] * 3
            for piece, index, step in plan.neighbours(cell):
                ref, fref, n = near[piece], flow[piece], ncell[piece]
                d = [shifted[f][step[f]] - row(ref, f * n + index) for f in range(3)]
                q = jnp.maximum(1.0 - (d[0] * d[0] + d[1] * d[1] + d[2] * d[2]), 0.0)
                q2 = q * q
                c = row(fref, 3 * n + index)
                p = (row(ref, 3 * n + index) * s + c) * q2
                w = c * (q2 * q)
                for f in range(3):
                    term = p * d[f] + w * (row(fref, f * n + index) - v[f])
                    total[f] = term if total[f] is None else total[f] + term
            for f in range(3):
                sums[f, at, :] = total[f]
            return carry

        lax.fori_loop(0, pl.cdiv(counts[o], SUB), chunk, 0)
        for f in range(3):
            accel[pl.ds(f * owns + o, 1), :] = jnp.sum(sums[f].T, axis=0, keepdims=True)


def call(kernel, out_rows, slots, args, scratch):
    vmem = pl.BlockSpec(memory_space=pltpu.VMEM)
    smem = pl.BlockSpec(memory_space=pltpu.SMEM)
    return pl.pallas_call(
        kernel,
        out_shape=jax.ShapeDtypeStruct((out_rows, slots), jnp.float32),
        in_specs=[smem, smem] + [vmem] * (len(args) - 2),
        out_specs=vmem,
        scratch_shapes=scratch,
        compiler_params=pltpu.CompilerParams(vmem_limit_bytes=16 << 20),
    )(*args)


def local(sizes, offsets, velocity, mass, counts):
    slots = offsets.shape[-1]
    extents = offsets.shape[1:4]
    plan = Plan(sizes, extents)
    owns = len(plan.own)
    axes = ("gx", "gy", "gz")
    odd = [lax.axis_index(a) % 2 for a in axes]
    info = jnp.stack([1 - 2 * o for o in odd]).astype(jnp.int32)

    def orient(cells, first):
        for k in range(3):
            cells = jnp.where(odd[k] == 1, jnp.flip(cells, first + k), cells)
        return cells

    def valid_of(axis, kind):
        i, n = lax.axis_index(axis), sizes[axis]
        if kind == "A":
            return (i ^ 1) < n
        return (i > 0) & (((i - 1) ^ 1) + 1 < n)

    def masked(cells, axis, dim):
        size = cells.shape[dim] - len(kinds_of(sizes[axis]))
        at = lax.broadcasted_iota(jnp.int32, cells.shape, dim)
        keep = at < size
        for k, kind in enumerate(kinds_of(sizes[axis])):
            keep |= (at == size + k) & valid_of(axis, kind)
        field = lax.broadcasted_iota(jnp.int32, cells.shape, 0)
        return jnp.where(keep | (field != 3), cells, 0.0)

    slot = lax.broadcasted_iota(jnp.int32, counts.shape + (slots,), 3)
    occupied = slot < counts[..., None]
    heavy = jnp.where(occupied, mass * KERNEL_NORM, 0.0)
    state = orient(jnp.concatenate([offsets, heavy[None]], axis=0), 1)
    own_counts = orient(counts, 0).reshape(owns)

    def gather(state):
        block = masked(extend(state, sizes, "gx", 1), "gx", 1)
        block = masked(extend(block, sizes, "gy", 2), "gy", 2)
        sides = []
        for kind in ("A", "B"):
            at = plan.lz - 1 if kind == "A" else 0
            message = lax.slice_in_dim(block, at, at + 1, axis=3)
            if kind in kinds_of(sizes["gz"]):
                side = swap(message, sizes, "gz", kind)
                field = lax.broadcasted_iota(jnp.int32, side.shape, 0)
                side = jnp.where((field != 3) | valid_of("gz", kind), side, 0.0)
            else:
                side = jnp.zeros_like(message)
            sides.append(side.reshape(-1, slots))
        return [block.reshape(-1, slots)] + sides

    near = gather(state)
    f32 = jnp.float32
    raw = call(
        functools.partial(density_kernel, plan),
        owns, slots, [info, own_counts] + near,
        [pltpu.VMEM((3, slots, slots), f32), pltpu.VMEM((slots, slots), f32)],
    ).reshape(extents + (slots,))
    full = orient(occupied, 0)
    density = jnp.where(full, raw, 0.0)
    rho = jnp.where(full, raw, 1.0)
    press = PRESSURE_COEF / rho
    share = state[3] * VISCOSITY / rho
    flow = jnp.concatenate([orient(velocity, 1) * (1.0 / 6.0), share[None]], axis=0)
    flow_near = gather(flow)
    force = call(
        functools.partial(force_kernel, plan),
        3 * owns, slots, [info, own_counts] + near + flow_near + [press.reshape(owns, slots)],
        [pltpu.VMEM((7, slots, slots), f32), pltpu.VMEM((3, slots, slots), f32)],
    ).reshape((3,) + tuple(extents) + (slots,))
    accel = jnp.where(full[None], force * 6.0, 0.0)
    return orient(accel, 1), orient(density, 0)


def solution(mesh):
    sizes = dict(mesh.shape)
    in_specs = (
        P(None, "gx", "gy", "gz", None),
        P(None, "gx", "gy", "gz", None),
        P("gx", "gy", "gz", None),
        P("gx", "gy", "gz"),
    )
    out_specs = (P(None, "gx", "gy", "gz", None), P("gx", "gy", "gz", None))
    return jax.shard_map(
        functools.partial(local, sizes), mesh=mesh, in_specs=in_specs, out_specs=out_specs, check_vma=False
    )
```

```python
import functools
import math

import jax
import jax.numpy as jnp
from jax import lax
from jax.experimental import pallas as pl
from jax.experimental.pallas import tpu as pltpu
from jax.sharding import PartitionSpec as P

KERNEL_NORM = 315.0 / (64.0 * math.pi)
PRESSURE_COEF = 0.5
SUB = 8


def partner_pairs(sizes, axis, kind):
    n, nx = sizes[axis], sizes["gx"]
    pairs = []
    for i in range(n):
        j = (i ^ 1) if kind == "A" else ((i - 1) ^ 1) + 1
        if i == 0 and kind == "B" or j >= n or j < 0:
            j = i
        pairs.append(j)
    if axis == "gx":
        if kind == "B":
            pairs[0], pairs[n - 1] = n - 1, 0
        return "gx", [(i, j) for i, j in enumerate(pairs)]
    if all(i != j for i, j in enumerate(pairs)):
        return axis, list(enumerate(pairs))
    out = []
    for x in range(nx):
        for i, j in enumerate(pairs):
            to = (x, j)
            if i == j and nx % 2 == 0:
                to = (x ^ 1, j)
            out.append((x * n + i, to[0] * n + to[1]))
    return ("gx", axis), out


def swap(message, sizes, axis, kind):
    names, pairs = partner_pairs(sizes, axis, kind)
    return lax.ppermute(message, names, pairs)


def kinds_of(n):
    return ("A", "B") if n > 2 else ("A",) if n > 1 else ()


def extend(cells, sizes, axis, dim):
    size = cells.shape[dim]
    parts = [cells]
    for kind in kinds_of(sizes[axis]):
        at = size - 1 if kind == "A" else 0
        parts.append(swap(lax.slice_in_dim(cells, at, at + 1, axis=dim), sizes, axis, kind))
    return jnp.concatenate(parts, axis=dim)


def order_of(size, n):
    return list(range(1, size + 1)) + [{"A": size + 1, "B": 0}[k] for k in kinds_of(n)]


class Plan:
    def __init__(self, sizes, extents, slots):
        self.sizes, self.extents, self.slots = sizes, extents, slots
        self.lx, self.ly, self.lz = extents
        self.X = order_of(self.lx, sizes["gx"])
        self.Y = order_of(self.ly, sizes["gy"])
        self.columns = len(self.X) * len(self.Y)
        self.cells = self.columns * self.lz
        self.own_columns = [(x, y) for x in range(1, self.lx + 1) for y in range(1, self.ly + 1)]
        self.own_cells = [(x, y, z) for x, y in self.own_columns for z in range(1, self.lz + 1)]
        self.owns = len(self.own_cells)

    def column_index(self, x, y):
        return self.X.index(x) * len(self.Y) + self.Y.index(y)

    def cell_index(self, x, y, z):
        return self.column_index(x, y) * self.lz + z - 1

    def near_columns(self, x, y):
        return [
            self.column_index(x + a, y + b)
            for a in (-1, 0, 1)
            for b in (-1, 0, 1)
            if x + a in self.X and y + b in self.Y
        ]

    def near_cells(self, x, y, z):
        return [k * self.lz + c - 1 for k in self.near_columns(x, y) for c in (z - 1, z, z + 1) if 1 <= c <= self.lz]

    def near_sides(self, x, y, z):
        sides = [side for side in range(2) if z == (self.lz if side == 0 else 1)]
        return [side * self.columns + k for side in sides for k in self.near_columns(x, y)]


GROUPS_J = (0, 0, 1, 1, 0, 2)
GROUPS_I = (0, 1, 0, 1, 2, 0)
DEPTH = 32
ROWS = 16
BF16 = jnp.bfloat16
F32 = jnp.float32


def split3(x):
    high = x.astype(BF16).astype(F32)
    rest = x - high
    middle = rest.astype(BF16).astype(F32)
    return high, middle, rest - middle


def dot(a, b):
    return jnp.dot(a, b, preferred_element_type=F32)


def groups_of(rows):
    return [(a, min(SUB, rows - a)) for a in range(0, rows, SUB)]


def put_features(out, values, order, first, count):
    parts = [split3(v) for v in values]
    for group, which in enumerate(order):
        for r, part in enumerate(parts):
            out[pl.ds(first * DEPTH + group * len(values) + r, count, stride=DEPTH), :] = part[which]
    zero = jnp.zeros_like(values[0])
    for r in range(len(order) * len(values), DEPTH):
        out[pl.ds(first * DEPTH + r, count, stride=DEPTH), :] = zero


def near_features(x, y, z, g):
    return [g * (1.0 - (x * x + y * y + z * z)), -g, 2.0 * g * x, 2.0 * g * y, 2.0 * g * z]


AXES = ("gx", "gy", "gz")


class Places:
    def __init__(self, plan):
        self.mirrored, self.shift, self.inside = [], [], []
        for k, axis in enumerate(AXES):
            extent, n = plan.extents[k], plan.sizes[axis]
            i = lax.axis_index(axis)
            odd = lax.rem(i, 2) == 1
            self.mirrored.append(odd)
            sign = jnp.where(odd, -1.0, 1.0).astype(F32)
            self.shift.append([sign * (p - 0.5 * (extent + 1)) - 0.5 for p in range(extent + 2)])
            above = jnp.where(jnp.where(odd, i - 1, i + 1) < n, 1.0, 0.0).astype(F32)
            below = jnp.where(odd, jnp.where(i + 1 < n, 1.0, 0.0), jnp.where(i > 0, 1.0, 0.0)).astype(F32)
            self.inside.append([below] + [jnp.float32(1.0)] * extent + [above])

    def source(self, plan, cell):
        at = jnp.int32(0)
        for k in range(3):
            i, extent = cell[k] - 1, plan.extents[k]
            at = at * extent + jnp.where(self.mirrored[k], extent - 1 - i, i)
        return at


def pattern(values, period, slots):
    at = lax.broadcasted_iota(jnp.int32, (len(values) * period, slots), 0)
    out = jnp.full(at.shape, values[0])
    for r in range(1, len(values)):
        out = jnp.where(at >= r * period, values[r], out)
    return out


def place_cells(plan, places, ref, out, xs, ys, zs):
    slots, rows = plan.slots, len(ys) * len(zs)
    cells = rows * len(xs)
    shift_y = pattern([places.shift[1][y] for y in ys], len(zs), slots)
    keep_y = pattern([places.inside[1][y] for y in ys], len(zs), slots)
    if len(zs) == 1:
        shift_z, keep_z = places.shift[2][zs[0]], places.inside[2][zs[0]]
    else:
        at = lax.rem(lax.broadcasted_iota(jnp.int32, (rows, slots), 0), len(zs))
        shift_z, keep_z = jnp.full(at.shape, places.shift[2][zs[0]]), 1.0
        for r in range(1, len(zs)):
            shift_z = jnp.where(at == r, places.shift[2][zs[r]], shift_z)
    keep_yz = keep_y * keep_z
    for g, x in enumerate(xs):
        at = [pl.ds(f * cells + g * rows, rows) for f in range(4)]
        out[at[0], :] = ref[at[0], :] + places.shift[0][x]
        out[at[1], :] = ref[at[1], :] + shift_y
        out[at[2], :] = ref[at[2], :] + shift_z
        out[at[3], :] = ref[at[3], :] * (keep_yz * places.inside[0][x])


def own_range(plan, k):
    return list(range(1, plan.extents[k] + 1))


def numbers_of(state, plan):
    full = jnp.where(state[pl.ds(3 * plan.owns, plan.owns), :] > 0.0, 1.0, 0.0)
    return [jnp.sum(full[o : o + 1, :]).astype(jnp.int32) for o in range(plan.owns)]


def near_operand(staged, left, ref, cells, first):
    slots = ref.shape[1]
    for start, count in groups_of(cells):
        values = near_features(*(ref[pl.ds(f * cells + start, count), :] for f in range(4)))
        put_features(staged, values, GROUPS_J, first + start, count)
    for c in range(first, first + cells):
        left[pl.ds(c * slots, slots), :] = staged[pl.ds(c * DEPTH, DEPTH), :].T.astype(BF16)


def prepare_kernel(plan, fields, state, speed):
    owns, slots = plan.owns, plan.slots
    places = Places(plan)
    for o, cell in enumerate(plan.own_cells):
        at = places.source(plan, cell)
        for f in range(3):
            state[pl.ds(f * owns + o, 1), :] = fields[pl.ds(f * owns + at, 1), :]
        speed[pl.ds(3 * owns + o, 1), :] = fields[pl.ds(7 * owns + at, 1), :]
        state[pl.ds(3 * owns + o, 1), :] = fields[pl.ds(6 * owns + at, 1), :]
    heavy = state[pl.ds(3 * owns, owns), :] * KERNEL_NORM
    root = jnp.exp(jnp.log(heavy) * (1.0 / 3.0))
    root = root * (2.0 / 3.0) + heavy / (3.0 * root * root)
    lane = lax.broadcasted_iota(jnp.int32, (owns, slots), 1).astype(F32)
    state[pl.ds(3 * owns, owns), :] = jnp.where(lane < speed[pl.ds(3 * owns, owns), :], root, 0.0)
    for o, cell in enumerate(plan.own_cells):
        at = places.source(plan, cell)
        for f in range(3):
            speed[pl.ds(f * owns + o, 1), :] = fields[pl.ds((3 + f) * owns + at, 1), :] * (1.0 / 6.0)


def cubes(left, right):
    q = jnp.maximum(dot(left, right), 0.0)
    return jnp.sum((q * q * q).reshape(q.shape[0] // SUB, SUB, q.shape[1]), axis=0)


def density_block_kernel(plan, raw, cells, right, sums, staged, own, left):
    slots = plan.slots
    place_cells(plan, Places(plan), raw, cells, plan.X, plan.Y, own_range(plan, 2))
    near_operand(staged, left, cells, plan.cells, 0)
    for p, (x, y) in enumerate(plan.own_columns):
        for z in range(plan.lz):
            c = plan.cell_index(x, y, z + 1)
            line = [cells[pl.ds(f * plan.cells + c, 1), :] for f in range(3)]
            values = [jnp.ones_like(line[0]), line[0] * line[0] + line[1] * line[1] + line[2] * line[2], *line]
            put_features(own, values, GROUPS_I, 0, 1)
            right[p, :, pl.ds(z * slots, slots)] = own[...].astype(BF16)
    for p, (x, y) in enumerate(plan.own_columns):
        mine = right[p]
        total = jnp.zeros((SUB, plan.lz * slots), F32)
        for k in plan.near_columns(x, y):
            total += cubes(left[pl.ds(k * plan.lz * slots, plan.lz * slots), :], mine)
        sums[p] = total


def density_side_kernel(
    plan, raw_a, raw_b, state, speed, right, sums, za, zb, flow, density, staged, left
):
    slots, n, owns = plan.slots, plan.columns, plan.owns
    places = Places(plan)
    for side, (raw, ref) in enumerate(((raw_a, za), (raw_b, zb))):
        place_cells(plan, places, raw, ref, plan.X, plan.Y, [plan.lz + 1 if side == 0 else 0])
        near_operand(staged, left, ref, n, side * n)
    flow[pl.ds(0, 3 * owns), :] = speed[pl.ds(0, 3 * owns), :]
    for o, (x, y, z) in enumerate(plan.own_cells):
        p = plan.own_columns.index((x, y))
        lanes = pl.ds((z - 1) * slots, slots)
        total = sums[p, :, lanes]
        mine = right[p, :, lanes]
        for c in plan.near_sides(x, y, z):
            total += cubes(left[pl.ds(c * slots, slots), :], mine)
        total = jnp.sum(total, axis=0, keepdims=True)
        full = state[pl.ds(3 * owns + o, 1), :] > 0.0
        density[pl.ds(places.source(plan, (x, y, z)), 1), :] = jnp.where(full, total, 0.0)
        flow[pl.ds(3 * owns + o, 1), :] = PRESSURE_COEF / jnp.where(full, total, 1.0)


def force_rows(out, ref, flow, cells, first):
    for start, count in groups_of(cells):
        g = ref[pl.ds(3 * cells + start, count), :]
        m = g * g * g
        out[0, pl.ds(first + start, count), :] = m
        out[1, pl.ds(first + start, count), :] = m * flow[pl.ds(3 * cells + start, count), :]


def line_of(ref, row):
    return ref[pl.ds(row, SUB, stride=0), :]


def force_pairs(count, near, columns, o, start, sums):
    def step(i, carry):
        base = pl.multiple_of(i * ROWS, ROWS)
        at = [pl.ds(base + r, SUB) for r in range(0, ROWS, SUB)]
        own = [[columns[f, o, a, :] for f in range(4)] for a in at]
        total = [[None] * 4 for _ in at] if start is None else [[start[k, o, a, :] for k in range(4)] for a in at]
        add = lambda old, new: new if old is None else old + new
        for lines in near:
            x, y, z, m, c, vx, vy, vz = lines()
            for r in range(len(at)):
                d = [own[r][0] - x, own[r][1] - y, own[r][2] - z]
                q = jnp.maximum(1.0 - (d[0] * d[0] + d[1] * d[1] + d[2] * d[2]), 0.0)
                q2 = q * q
                p = (m * own[r][3] + c) * q2
                w = c * (q2 * q)
                total[r][3] = add(total[r][3], w)
                for f, v in enumerate((vx, vy, vz)):
                    total[r][f] = add(total[r][f], p * d[f] + w * v)
        for r, a in enumerate(at):
            for k in range(4):
                sums[k, o, a, :] = total[r][k]
        return carry

    lax.fori_loop(0, lax.div(count + (ROWS - 1), ROWS), step, 0)


def lines_from(ref, flow, extra, cells, c, e):
    return lambda: (
        *(line_of(ref, f * cells + c) for f in range(3)),
        *(line_of(extra.at[k], e) for k in range(2)),
        *(line_of(flow, f * cells + c) for f in range(3)),
    )


def force_own_kernel(plan, cells, flow, columns, sums, extra, placed):
    slots, owns = plan.slots, plan.owns
    numbers = numbers_of(cells, plan)
    place_cells(plan, Places(plan), cells, placed, *(own_range(plan, k) for k in range(3)))
    rows = [placed[pl.ds(0, 3 * owns), :], flow[pl.ds(3 * owns, owns), :], jnp.zeros((slots - 4 * owns, slots), F32)]
    table = jnp.concatenate(rows, axis=0).T
    for f in range(4):
        for o in range(owns):
            e = f * owns + o
            columns[f, o] = jnp.broadcast_to(table[:, e : e + 1], (slots, slots))
    force_rows(extra, placed, flow, owns, 0)
    for o, cell in enumerate(plan.own_cells):
        near = [
            lines_from(placed, flow, extra, owns, c, c)
            for c, other in enumerate(plan.own_cells)
            if max(abs(p - q) for p, q in zip(cell, other)) <= 1
        ]
        force_pairs(numbers[o], near, columns, o, None, sums)


def force_block_kernel(plan, state, cells, flow, columns, start, sums, extra):
    numbers = numbers_of(state, plan)
    force_rows(extra, cells, flow, plan.cells, 0)
    own = [plan.cell_index(*cell) for cell in plan.own_cells]
    for o, (x, y, z) in enumerate(plan.own_cells):
        near = [
            lines_from(cells, flow, extra, plan.cells, c, c) for c in plan.near_cells(x, y, z) if c not in own
        ]
        force_pairs(numbers[o], near, columns, o, start, sums)


def force_side_kernel(plan, state, flow, za, zb, fza, fzb, columns, start, accel, sums, extra):
    slots, n, owns = plan.slots, plan.columns, plan.owns
    numbers = numbers_of(state, plan)
    places = Places(plan)
    for side, (ref, fref) in enumerate(((za, fza), (zb, fzb))):
        force_rows(extra, ref, fref, n, side * n)
    for o, (x, y, z) in enumerate(plan.own_cells):
        near = []
        for e in plan.near_sides(x, y, z):
            side, k = divmod(e, n)
            near.append(lines_from((za, zb)[side], (fza, fzb)[side], extra, n, k, e))
        force_pairs(numbers[o], near, columns, o, start, sums)
    lane = lax.broadcasted_iota(jnp.int32, (slots, slots), 1)
    table = jnp.zeros((slots, slots), F32)
    for e in range(4 * owns):
        table = jnp.where(lane == e, jnp.sum(sums[e // owns, e % owns], axis=1, keepdims=True), table)
    whole = table.T
    for o, cell in enumerate(plan.own_cells):
        at = places.source(plan, cell)
        full = state[pl.ds(3 * owns + o, 1), :] > 0.0
        for f in range(3):
            v = flow[pl.ds(f * owns + o, 1), :]
            value = 6.0 * (whole[f * owns + o : f * owns + o + 1] - v * whole[3 * owns + o : 3 * owns + o + 1])
            accel[pl.ds(f * owns + at, 1), :] = jnp.where(full, value, 0.0)


def call(kernel, args, outs, scratch, cost, aliases=None):
    vmem = pl.BlockSpec(memory_space=pltpu.VMEM)
    return pl.pallas_call(
        kernel,
        out_shape=[jax.ShapeDtypeStruct(shape, dtype) for shape, dtype in outs],
        in_specs=[vmem] * len(args),
        out_specs=[vmem] * len(outs),
        scratch_shapes=scratch,
        input_output_aliases=aliases or {},
        cost_estimate=pl.CostEstimate(flops=cost, bytes_accessed=1 << 20, transcendentals=0),
        compiler_params=pltpu.CompilerParams(vmem_limit_bytes=16 << 20),
    )(*args)


def local(sizes, offsets, velocity, mass, counts):
    slots = offsets.shape[-1]
    extents = offsets.shape[1:4]
    plan = Plan(sizes, extents, slots)
    pairs, lz, total, columns, owns = len(plan.own_columns), plan.lz, plan.cells, plan.columns, plan.owns
    flat = lambda cells: cells.reshape(-1, slots)

    def gather(state):
        block = extend(state.reshape((4,) + extents + (slots,)), sizes, "gx", 1)
        block = extend(block, sizes, "gy", 2)
        sides = []
        for kind in ("A", "B"):
            at = lz - 1 if kind == "A" else 0
            message = lax.slice_in_dim(block, at, at + 1, axis=3)
            present = kind in kinds_of(sizes["gz"])
            sides.append(flat(swap(message, sizes, "gz", kind) if present else jnp.zeros_like(message)))
        return flat(block), sides

    number = jnp.broadcast_to(counts.astype(F32)[..., None], mass.shape)
    fields = flat(jnp.concatenate([offsets, velocity, mass[None], number[None]], axis=0))
    state, speed = call(
        functools.partial(prepare_kernel, plan),
        [fields],
        [((4 * owns, slots), F32), ((4 * owns, slots), F32)],
        [],
        1 << 20,
    )
    raw, (raw_a, raw_b) = gather(state)
    cells, right, sums = call(
        functools.partial(density_block_kernel, plan),
        [raw],
        [
            ((4 * total, slots), F32),
            ((pairs, DEPTH, lz * slots), BF16),
            ((pairs, SUB, lz * slots), F32),
        ],
        [
            pltpu.VMEM((total * DEPTH, slots), F32),
            pltpu.VMEM((DEPTH, slots), F32),
            pltpu.VMEM((total * slots, DEPTH), BF16),
        ],
        1 << 27,
    )
    side = ((4 * columns, slots), F32)
    za, zb, flow_state, density = call(
        functools.partial(density_side_kernel, plan),
        [raw_a, raw_b, state, speed, right, sums],
        [side, side, ((4 * owns, slots), F32), ((owns, slots), F32)],
        [pltpu.VMEM((2 * columns * DEPTH, slots), F32), pltpu.VMEM((2 * columns * slots, DEPTH), BF16)],
        1 << 26,
    )
    flow, (fza, fzb) = gather(flow_state)
    wide = (4, owns, slots, slots)
    repeated, partial = call(
        functools.partial(force_own_kernel, plan),
        [state, flow_state],
        [(wide, F32), (wide, F32)],
        [pltpu.VMEM((2, owns, slots), F32), pltpu.VMEM((4 * owns, slots), F32)],
        1 << 27,
    )
    (partial,) = call(
        functools.partial(force_block_kernel, plan),
        [state, cells, flow, repeated, partial],
        [(wide, F32)],
        [pltpu.VMEM((2, total, slots), F32)],
        1 << 27,
        {4: 0},
    )
    (force,) = call(
        functools.partial(force_side_kernel, plan),
        [state, flow_state, za, zb, fza, fzb, repeated, partial],
        [((3 * owns, slots), F32)],
        [pltpu.VMEM(wide, F32), pltpu.VMEM((2, 2 * columns, slots), F32)],
        1 << 27,
    )
    return force.reshape(offsets.shape), density.reshape(mass.shape)


def layer(sizes, *args):
    return local(sizes, *args)


def solution(mesh):
    sizes = dict(mesh.shape)
    in_specs = (
        P(None, "gx", "gy", "gz", None),
        P(None, "gx", "gy", "gz", None),
        P("gx", "gy", "gz", None),
        P("gx", "gy", "gz"),
    )
    out_specs = (P(None, "gx", "gy", "gz", None), P("gx", "gy", "gz", None))
    return jax.shard_map(
        functools.partial(layer, sizes), mesh=mesh, in_specs=in_specs, out_specs=out_specs, check_vma=False
    )
```

```python
import functools
import math

import jax
import jax.numpy as jnp
from jax import lax
from jax.experimental import pallas as pl
from jax.experimental.pallas import tpu as pltpu
from jax.sharding import PartitionSpec as P

KERNEL_NORM = 315.0 / (64.0 * math.pi)
PRESSURE_COEF = 0.5
SUB = 8


def partner_pairs(sizes, axis, kind):
    n, nx = sizes[axis], sizes["gx"]
    pairs = []
    for i in range(n):
        j = (i ^ 1) if kind == "A" else ((i - 1) ^ 1) + 1
        if i == 0 and kind == "B" or j >= n or j < 0:
            j = i
        pairs.append(j)
    if axis == "gx":
        if kind == "B":
            pairs[0], pairs[n - 1] = n - 1, 0
        return "gx", [(i, j) for i, j in enumerate(pairs)]
    if all(i != j for i, j in enumerate(pairs)):
        return axis, list(enumerate(pairs))
    out = []
    for x in range(nx):
        for i, j in enumerate(pairs):
            to = (x, j)
            if i == j and nx % 2 == 0:
                to = (x ^ 1, j)
            out.append((x * n + i, to[0] * n + to[1]))
    return ("gx", axis), out


def swap(message, sizes, axis, kind):
    names, pairs = partner_pairs(sizes, axis, kind)
    return lax.ppermute(message, names, pairs)


def kinds_of(n):
    return ("A", "B") if n > 2 else ("A",) if n > 1 else ()


def extend(cells, sizes, axis, dim):
    size = cells.shape[dim]
    parts = [cells]
    for kind in kinds_of(sizes[axis]):
        at = size - 1 if kind == "A" else 0
        parts.append(swap(lax.slice_in_dim(cells, at, at + 1, axis=dim), sizes, axis, kind))
    return jnp.concatenate(parts, axis=dim)


def order_of(size, n):
    return list(range(1, size + 1)) + [{"A": size + 1, "B": 0}[k] for k in kinds_of(n)]


class Plan:
    def __init__(self, sizes, extents, slots):
        self.sizes, self.extents, self.slots = sizes, extents, slots
        self.lx, self.ly, self.lz = extents
        self.X = order_of(self.lx, sizes["gx"])
        self.Y = order_of(self.ly, sizes["gy"])
        self.columns = len(self.X) * len(self.Y)
        self.cells = self.columns * self.lz
        self.own_columns = [(x, y) for x in range(1, self.lx + 1) for y in range(1, self.ly + 1)]
        self.own_cells = [(x, y, z) for x, y in self.own_columns for z in range(1, self.lz + 1)]
        self.owns = len(self.own_cells)

    def column_index(self, x, y):
        return self.X.index(x) * len(self.Y) + self.Y.index(y)

    def cell_index(self, x, y, z):
        return self.column_index(x, y) * self.lz + z - 1

    def near_columns(self, x, y):
        return [
            self.column_index(x + a, y + b)
            for a in (-1, 0, 1)
            for b in (-1, 0, 1)
            if x + a in self.X and y + b in self.Y
        ]

    def near_cells(self, x, y, z):
        return [k * self.lz + c - 1 for k in self.near_columns(x, y) for c in (z - 1, z, z + 1) if 1 <= c <= self.lz]

    def beside(self, side):
        z = self.lz if side == 0 else 1
        return [(o, cell) for o, cell in enumerate(self.own_cells) if cell[2] == z]

    def lanes(self, cell):
        return self.own_columns.index(cell[:2]), pl.ds((cell[2] - 1) * self.slots, self.slots)


GROUPS_J = (0, 0, 1, 1, 0, 2)
GROUPS_I = (0, 1, 0, 1, 2, 0)
DEPTH = 32
ROWS = 16
BF16 = jnp.bfloat16
F32 = jnp.float32


def split3(x):
    high = x.astype(BF16).astype(F32)
    rest = x - high
    middle = rest.astype(BF16).astype(F32)
    return high, middle, rest - middle


def dot(a, b):
    return jnp.dot(a, b, preferred_element_type=F32)


def groups_of(rows):
    return [(a, min(SUB, rows - a)) for a in range(0, rows, SUB)]


def put_features(out, values, order, first, count):
    parts = [split3(v) for v in values]
    for group, which in enumerate(order):
        for r, part in enumerate(parts):
            out[pl.ds(first * DEPTH + group * len(values) + r, count, stride=DEPTH), :] = part[which]
    zero = jnp.zeros_like(values[0])
    for r in range(len(order) * len(values), DEPTH):
        out[pl.ds(first * DEPTH + r, count, stride=DEPTH), :] = zero


def near_features(x, y, z, g):
    return [g * (1.0 - (x * x + y * y + z * z)), -g, 2.0 * g * x, 2.0 * g * y, 2.0 * g * z]


AXES = ("gx", "gy", "gz")


class Places:
    def __init__(self, plan):
        self.mirrored, self.shift, self.inside = [], [], []
        for k, axis in enumerate(AXES):
            extent, n = plan.extents[k], plan.sizes[axis]
            i = lax.axis_index(axis)
            odd = lax.rem(i, 2) == 1
            self.mirrored.append(odd)
            sign = jnp.where(odd, -1.0, 1.0).astype(F32)
            self.shift.append([sign * (p - 0.5 * (extent + 1)) - 0.5 for p in range(extent + 2)])
            above = jnp.where(jnp.where(odd, i - 1, i + 1) < n, 1.0, 0.0).astype(F32)
            below = jnp.where(odd, jnp.where(i + 1 < n, 1.0, 0.0), jnp.where(i > 0, 1.0, 0.0)).astype(F32)
            self.inside.append([below] + [jnp.float32(1.0)] * extent + [above])

    def source_position(self, plan, cell):
        return [jnp.where(self.mirrored[k], plan.extents[k] - cell[k], cell[k] - 1) for k in range(3)]

    def source(self, plan, cell):
        x, y, z = self.source_position(plan, cell)
        return (x * plan.extents[1] + y) * plan.extents[2] + z


def pattern(values, period, slots):
    at = lax.broadcasted_iota(jnp.int32, (len(values) * period, slots), 0)
    out = jnp.full(at.shape, values[0])
    for r in range(1, len(values)):
        out = jnp.where(at >= r * period, values[r], out)
    return out


def place_cells(plan, places, ref, out, xs, ys, zs):
    slots, rows = plan.slots, len(ys) * len(zs)
    cells = rows * len(xs)
    shift_y = pattern([places.shift[1][y] for y in ys], len(zs), slots)
    keep_y = pattern([places.inside[1][y] for y in ys], len(zs), slots)
    if len(zs) == 1:
        shift_z, keep_z = places.shift[2][zs[0]], places.inside[2][zs[0]]
    else:
        at = lax.rem(lax.broadcasted_iota(jnp.int32, (rows, slots), 0), len(zs))
        shift_z, keep_z = jnp.full(at.shape, places.shift[2][zs[0]]), 1.0
        for r in range(1, len(zs)):
            shift_z = jnp.where(at == r, places.shift[2][zs[r]], shift_z)
    keep_yz = keep_y * keep_z
    for g, x in enumerate(xs):
        at = [pl.ds(f * cells + g * rows, rows) for f in range(4)]
        out[at[0], :] = ref[at[0], :] + places.shift[0][x]
        out[at[1], :] = ref[at[1], :] + shift_y
        out[at[2], :] = ref[at[2], :] + shift_z
        out[at[3], :] = ref[at[3], :] * (keep_yz * places.inside[0][x])


def own_range(plan, k):
    return list(range(1, plan.extents[k] + 1))


def numbers_of(state, plan):
    full = jnp.where(state[pl.ds(3 * plan.owns, plan.owns), :] > 0.0, 1.0, 0.0)
    return [jnp.sum(full[o : o + 1, :]).astype(jnp.int32) for o in range(plan.owns)]


def near_operand(staged, left, ref, cells, first):
    slots = ref.shape[1]
    for start, count in groups_of(cells):
        values = near_features(*(ref[pl.ds(f * cells + start, count), :] for f in range(4)))
        put_features(staged, values, GROUPS_J, first + start, count)
    for c in range(first, first + cells):
        left[pl.ds(c * slots, slots), :] = staged[pl.ds(c * DEPTH, DEPTH), :].T.astype(BF16)


def prepare_kernel(plan, fields, counts, state, speed):
    owns, slots = plan.owns, plan.slots
    places = Places(plan)
    row = lax.broadcasted_iota(jnp.int32, plan.extents[1:], 0)
    column = lax.broadcasted_iota(jnp.int32, plan.extents[1:], 1)
    line = lax.broadcasted_iota(jnp.int32, (owns, slots), 0)
    held = jnp.zeros((owns, slots), F32)
    for o, cell in enumerate(plan.own_cells):
        at = places.source(plan, cell)
        x, y, z = places.source_position(plan, cell)
        number = jnp.sum(jnp.where((row == y) & (column == z), counts[x].astype(F32), 0.0))
        held = jnp.where(line == o, number, held)
        for f in range(3):
            state[pl.ds(f * owns + o, 1), :] = fields[pl.ds(f * owns + at, 1), :]
        state[pl.ds(3 * owns + o, 1), :] = fields[pl.ds(6 * owns + at, 1), :]
    heavy = state[pl.ds(3 * owns, owns), :] * KERNEL_NORM
    root = jnp.exp(jnp.log(heavy) * (1.0 / 3.0))
    root = root * (2.0 / 3.0) + heavy / (3.0 * root * root)
    lane = lax.broadcasted_iota(jnp.int32, (owns, slots), 1).astype(F32)
    state[pl.ds(3 * owns, owns), :] = jnp.where(lane < held, root, 0.0)
    for o, cell in enumerate(plan.own_cells):
        at = places.source(plan, cell)
        for f in range(3):
            speed[pl.ds(f * owns + o, 1), :] = fields[pl.ds((3 + f) * owns + at, 1), :] * (1.0 / 6.0)


def cubes(left, right):
    q = jnp.maximum(dot(left, right), 0.0)
    return jnp.sum((q * q * q).reshape(q.shape[0] // SUB, SUB, q.shape[1]), axis=0)


def density_block_kernel(plan, raw, cells, right, sums, staged, own, left):
    slots = plan.slots
    place_cells(plan, Places(plan), raw, cells, plan.X, plan.Y, own_range(plan, 2))
    near_operand(staged, left, cells, plan.cells, 0)
    for p, (x, y) in enumerate(plan.own_columns):
        for z in range(plan.lz):
            c = plan.cell_index(x, y, z + 1)
            line = [cells[pl.ds(f * plan.cells + c, 1), :] for f in range(3)]
            values = [jnp.ones_like(line[0]), line[0] * line[0] + line[1] * line[1] + line[2] * line[2], *line]
            put_features(own, values, GROUPS_I, 0, 1)
            right[p, :, pl.ds(z * slots, slots)] = own[...].astype(BF16)
    for p, (x, y) in enumerate(plan.own_columns):
        mine = right[p]
        total = jnp.zeros((SUB, plan.lz * slots), F32)
        for k in plan.near_columns(x, y):
            total += cubes(left[pl.ds(k * plan.lz * slots, plan.lz * slots), :], mine)
        sums[p] = total


def density_side(plan, side, raw, placed, right, sums, staged, left):
    slots = plan.slots
    places = Places(plan)
    place_cells(plan, places, raw, placed, plan.X, plan.Y, [plan.lz + 1 if side == 0 else 0])
    near_operand(staged, left, placed, plan.columns, 0)
    out = {}
    for o, cell in plan.beside(side):
        p, lanes = plan.lanes(cell)
        total = sums[p, :, lanes]
        mine = right[p, :, lanes]
        for k in plan.near_columns(*cell[:2]):
            total += cubes(left[pl.ds(k * slots, slots), :], mine)
        out[o] = total
    return out


def density_above_kernel(plan, raw, right, sums, placed, out, staged, left):
    done = density_side(plan, 0, raw, placed, right, sums, staged, left)
    for o, cell in enumerate(plan.own_cells):
        p, lanes = plan.lanes(cell)
        out[p, :, lanes] = done[o] if o in done else sums[p, :, lanes]


def density_below_kernel(plan, raw, state, speed, right, sums, placed, flow, density, staged, left):
    owns = plan.owns
    done = density_side(plan, 1, raw, placed, right, sums, staged, left)
    rows = []
    for o, cell in enumerate(plan.own_cells):
        p, lanes = plan.lanes(cell)
        rows.append(jnp.sum(done[o] if o in done else sums[p, :, lanes], axis=0, keepdims=True))
    total = jnp.concatenate(rows, axis=0)
    full = state[pl.ds(3 * owns, owns), :] > 0.0
    flow[pl.ds(0, 3 * owns), :] = speed[...]
    flow[pl.ds(3 * owns, owns), :] = PRESSURE_COEF / jnp.where(full, total, 1.0)
    density[...] = jnp.where(full, total, 0.0)


def gather_fields(out, near, flow, cells):
    for start, count in groups_of(cells):
        rows = [pl.ds(f * cells + start, count) for f in range(8)]
        g = near[rows[3], :]
        m = g * g * g
        for f in range(3):
            out[rows[f], :] = near[rows[f], :]
            out[rows[5 + f], :] = flow[rows[f], :]
        out[rows[3], :] = m
        out[rows[4], :] = m * flow[rows[3], :]


def pack(plan, fields, cells, chosen, counts, out):
    slots = plan.slots
    lane = lax.broadcasted_iota(jnp.int32, (SUB, slots), 1)
    size = jnp.int32(0)
    for c in chosen:
        edge = lax.rem(size, slots)
        block = lax.div(size, slots)
        moved = pltpu.roll(fields[pl.ds(c, SUB, stride=cells), :], edge, 1)
        out[block] = jnp.where(lane < edge, out[block], moved)
        out[block + 1] = jnp.where(lane < edge, moved, 0.0)
        size += counts[c]
    return lax.div(size + (slots - 1), slots)


def counts_of(fields, cells, chosen):
    return {c: jnp.sum(jnp.where(fields[pl.ds(3 * cells + c, 1), :] > 0.0, 1.0, 0.0)).astype(jnp.int32) for c in chosen}


def force_pairs(packed, blocks, limit, numbers, first, last, columns, press, sums, add):
    def with_blocks(used):
        def cell(o, carry):
            def step(i, inner):
                base = pl.multiple_of(i * ROWS, ROWS)
                at = [pl.ds(base + r, SUB) for r in range(0, ROWS, SUB)]
                own = [[*(columns[f, o, a, :] for f in range(3)), press[o, a, :]] for a in at]
                total = [[sums[k, o, a, :] for k in range(4)] if add else [None] * 4 for a in at]
                plus = lambda old, new: new if old is None else old + new
                for b in range(used):
                    x, y, z, m, c, *v = (packed[b, pl.ds(f, SUB, stride=0), :] for f in range(8))
                    for r in range(len(at)):
                        d = [own[r][0] - x, own[r][1] - y, own[r][2] - z]
                        q = jnp.maximum(1.0 - (d[0] * d[0] + d[1] * d[1] + d[2] * d[2]), 0.0)
                        q2 = q * q
                        p = (m * own[r][3] + c) * q2
                        w = c * (q2 * q)
                        total[r][3] = plus(total[r][3], w)
                        for f in range(3):
                            total[r][f] = plus(total[r][f], p * d[f] + w * v[f])
                for r, a in enumerate(at):
                    for k in range(4):
                        sums[k, o, a, :] = total[r][k]
                return inner

            lax.fori_loop(0, lax.div(numbers[o] + (ROWS - 1), ROWS), step, 0)
            return carry

        if last - first == 1:
            cell(first, 0)
        else:
            lax.fori_loop(first, last, cell, 0)

    for used in range(1, limit + 1):
        pl.when(blocks == used)(functools.partial(with_blocks, used))


def repeat(rows, out, slots):
    count = rows.shape[0]
    table = jnp.concatenate([rows, jnp.zeros((slots - count, slots), F32)], axis=0).T
    for e in range(count):
        out[e] = jnp.broadcast_to(table[:, e : e + 1], (slots, slots))


def repeat_places_kernel(plan, state, out, placed):
    place_cells(plan, Places(plan), state, placed, *(own_range(plan, k) for k in range(3)))
    for f in range(3):
        repeat(placed[pl.ds(f * plan.owns, plan.owns), :], out.at[f], plan.slots)


def repeat_press_kernel(plan, flow, density, out, ordered):
    places = Places(plan)
    for o, cell in enumerate(plan.own_cells):
        ordered[pl.ds(places.source(plan, cell), 1), :] = density[pl.ds(o, 1), :]
    repeat(flow[pl.ds(3 * plan.owns, plan.owns), :], out, plan.slots)


def note_numbers(plan, state, numbers):
    for o, number in enumerate(numbers_of(state, plan)):
        numbers[o] = number


def force_own_kernel(plan, cells, flow, columns, press, sums, fields, placed, packed, numbers):
    owns = plan.owns
    note_numbers(plan, cells, numbers)
    place_cells(plan, Places(plan), cells, placed, *(own_range(plan, k) for k in range(3)))
    gather_fields(fields, placed, flow, owns)
    chosen = list(range(owns))
    used = pack(plan, fields, owns, chosen, [numbers[o] for o in chosen], packed)
    force_pairs(packed, used, owns, numbers, 0, owns, columns, press, sums, False)


def force_block_kernel(plan, state, cells, flow, columns, press, start, sums, fields, packed, numbers):
    note_numbers(plan, state, numbers)
    gather_fields(fields, cells, flow, plan.cells)
    mine = [plan.column_index(x, y) for x, y in plan.own_columns]
    near = [
        [k * plan.lz + z for k in plan.near_columns(x, y) if k not in mine for z in range(plan.lz)]
        for x, y in plan.own_columns
    ]
    counts = counts_of(fields, plan.cells, sorted(set(sum(near, []))))
    used = [pack(plan, fields, plan.cells, chosen, counts, packed.at[p]) for p, chosen in enumerate(near)]
    for p, chosen in enumerate(near):
        first = p * plan.lz
        force_pairs(packed.at[p], used[p], len(chosen), numbers, first, first + plan.lz, columns, press, sums, True)


def force_side(plan, side, state, near, flow, columns, press, sums, fields, packed, numbers):
    n = plan.columns
    note_numbers(plan, state, numbers)
    gather_fields(fields, near, flow, n)
    counts = counts_of(fields, n, range(n))
    lists = [(o, plan.near_columns(*cell[:2])) for o, cell in plan.beside(side)]
    used = [pack(plan, fields, n, chosen, counts, packed.at[p]) for p, (_, chosen) in enumerate(lists)]
    for p, (o, chosen) in enumerate(lists):
        force_pairs(packed.at[p], used[p], len(chosen), numbers, o, o + 1, columns, press, sums, True)


def totals(plan, chosen, table):
    lane = lax.broadcasted_iota(jnp.int32, table.shape, 1)
    for o, sums in chosen:
        for k in range(4):
            table = jnp.where(lane == k * plan.owns + o, jnp.sum(sums[k, o], axis=1, keepdims=True), table)
    return table


def force_above_kernel(plan, state, near, flow, columns, press, start, sums, table, *scratch):
    force_side(plan, 0, state, near, flow, columns, press, sums, *scratch)
    mine = [] if plan.lz == 1 else [(o, sums) for o, _ in plan.beside(0)]
    table[...] = totals(plan, mine, jnp.zeros(table.shape, F32))


def force_below_kernel(plan, state, own, near, flow, columns, press, start, above, sums, accel, *scratch):
    owns = plan.owns
    force_side(plan, 1, state, near, flow, columns, press, sums, *scratch)
    known = [] if plan.lz == 1 else [o for o, _ in plan.beside(0)]
    mine = [(o, sums) for o in range(owns) if o not in known]
    whole = totals(plan, mine, above[...]).T
    places = Places(plan)
    full = state[pl.ds(3 * owns, owns), :] > 0.0
    for f in range(3):
        v = own[pl.ds(f * owns, owns), :]
        value = 6.0 * (whole[f * owns : (f + 1) * owns] - v * whole[3 * owns : 4 * owns])
        value = jnp.where(full, value, 0.0)
        for o, cell in enumerate(plan.own_cells):
            accel[pl.ds(f * owns + places.source(plan, cell), 1), :] = value[o : o + 1, :]


def call(kernel, args, outs, scratch, cost, aliases=None):
    vmem = pl.BlockSpec(memory_space=pltpu.VMEM)
    return pl.pallas_call(
        kernel,
        out_shape=[jax.ShapeDtypeStruct(shape, dtype) for shape, dtype in outs],
        in_specs=[vmem] * len(args),
        out_specs=[vmem] * len(outs),
        scratch_shapes=scratch,
        input_output_aliases=aliases or {},
        cost_estimate=pl.CostEstimate(flops=cost, bytes_accessed=1 << 20, transcendentals=0),
        compiler_params=pltpu.CompilerParams(vmem_limit_bytes=16 << 20),
    )(*args)


def local(sizes, offsets, velocity, mass, counts):
    slots = offsets.shape[-1]
    extents = offsets.shape[1:4]
    plan = Plan(sizes, extents, slots)
    pairs, lz, total, columns, owns = len(plan.own_columns), plan.lz, plan.cells, plan.columns, plan.owns
    flat = lambda cells: cells.reshape(-1, slots)

    def gather(state):
        block = extend(state.reshape((4,) + extents + (slots,)), sizes, "gx", 1)
        block = extend(block, sizes, "gy", 2)
        sides = []
        for kind in ("A", "B"):
            at = lz - 1 if kind == "A" else 0
            message = lax.slice_in_dim(block, at, at + 1, axis=3)
            present = kind in kinds_of(sizes["gz"])
            sides.append(flat(swap(message, sizes, "gz", kind) if present else jnp.zeros_like(message)))
        return flat(block), sides

    fields = flat(jnp.concatenate([offsets, velocity, mass[None]], axis=0))
    state, speed = call(
        functools.partial(prepare_kernel, plan),
        [fields, counts],
        [((4 * owns, slots), F32), ((3 * owns, slots), F32)],
        [],
        1 << 20,
    )
    wide = (owns, slots, slots)
    (places,) = call(
        functools.partial(repeat_places_kernel, plan),
        [state],
        [((3,) + wide, F32)],
        [pltpu.VMEM((4 * owns, slots), F32)],
        1 << 26,
    )
    raw, (raw_a, raw_b) = gather(state)
    cells, right, sums = call(
        functools.partial(density_block_kernel, plan),
        [raw],
        [
            ((4 * total, slots), F32),
            ((pairs, DEPTH, lz * slots), BF16),
            ((pairs, SUB, lz * slots), F32),
        ],
        [
            pltpu.VMEM((total * DEPTH, slots), F32),
            pltpu.VMEM((DEPTH, slots), F32),
            pltpu.VMEM((total * slots, DEPTH), BF16),
        ],
        1 << 27,
    )
    side = ((4 * columns, slots), F32)
    side_scratch = [pltpu.VMEM((columns * DEPTH, slots), F32), pltpu.VMEM((columns * slots, DEPTH), BF16)]
    za, sums = call(
        functools.partial(density_above_kernel, plan),
        [raw_a, right, sums],
        [side, ((pairs, SUB, lz * slots), F32)],
        side_scratch,
        1 << 25,
    )
    zb, flow_state, density = call(
        functools.partial(density_below_kernel, plan),
        [raw_b, state, speed, right, sums],
        [side, ((4 * owns, slots), F32), ((owns, slots), F32)],
        side_scratch,
        1 << 25,
    )
    flow, (fza, fzb) = gather(flow_state)
    press, density = call(
        functools.partial(repeat_press_kernel, plan),
        [flow_state, density],
        [(wide, F32), ((owns, slots), F32)],
        [],
        1 << 25,
    )
    four = ((4,) + wide, F32)
    numbers = pltpu.SMEM((owns,), jnp.int32)

    def scratch_of(cells, lists, most):
        return [pltpu.VMEM((8 * cells, slots), F32), pltpu.VMEM((*lists, most + 2, SUB, slots), F32), numbers]

    most = max(len(plan.near_columns(*cell[:2])) for cell in plan.own_cells)
    fields, packed, _ = scratch_of(owns, (), owns)
    (partial,) = call(
        functools.partial(force_own_kernel, plan),
        [state, flow_state, places, press],
        [four],
        [fields, pltpu.VMEM((4 * owns, slots), F32), packed, numbers],
        1 << 27,
    )
    (partial,) = call(
        functools.partial(force_block_kernel, plan),
        [state, cells, flow, places, press, partial],
        [four],
        scratch_of(total, (pairs,), most * lz),
        1 << 27,
        {5: 0},
    )
    partial, table = call(
        functools.partial(force_above_kernel, plan),
        [state, za, fza, places, press, partial],
        [four, ((slots, slots), F32)],
        scratch_of(columns, (pairs,), most),
        1 << 26,
        {5: 0},
    )
    _, force = call(
        functools.partial(force_below_kernel, plan),
        [state, flow_state, zb, fzb, places, press, partial, table],
        [four, ((3 * owns, slots), F32)],
        scratch_of(columns, (pairs,), most),
        1 << 26,
        {6: 0},
    )
    return force.reshape(offsets.shape), density.reshape(mass.shape)


def layer(sizes, *args):
    return local(sizes, *args)


def solution(mesh):
    sizes = dict(mesh.shape)
    in_specs = (
        P(None, "gx", "gy", "gz", None),
        P(None, "gx", "gy", "gz", None),
        P("gx", "gy", "gz", None),
        P("gx", "gy", "gz"),
    )
    out_specs = (P(None, "gx", "gy", "gz", None), P("gx", "gy", "gz", None))
    step = jax.shard_map(
        functools.partial(layer, sizes), mesh=mesh, in_specs=in_specs, out_specs=out_specs, check_vma=False
    )
    if min(sizes[a] for a in AXES) < 2:
        return step
    return step
```

```python
import functools
import math

import jax
import jax.numpy as jnp
from jax import lax
from jax.experimental import pallas as pl
from jax.experimental.pallas import tpu as pltpu
from jax.sharding import PartitionSpec as P

KERNEL_NORM = 315.0 / (64.0 * math.pi)
PRESSURE_COEF = 0.5
SUB = 8


def partner_pairs(sizes, axis, kind):
    n, nx = sizes[axis], sizes["gx"]
    pairs = []
    for i in range(n):
        j = (i ^ 1) if kind == "A" else ((i - 1) ^ 1) + 1
        if i == 0 and kind == "B" or j >= n or j < 0:
            j = i
        pairs.append(j)
    if axis == "gx":
        if kind == "B":
            pairs[0], pairs[n - 1] = n - 1, 0
        return "gx", [(i, j) for i, j in enumerate(pairs)]
    if all(i != j for i, j in enumerate(pairs)):
        return axis, list(enumerate(pairs))
    out = []
    for x in range(nx):
        for i, j in enumerate(pairs):
            to = (x, j)
            if i == j and nx % 2 == 0:
                to = (x ^ 1, j)
            out.append((x * n + i, to[0] * n + to[1]))
    return ("gx", axis), out


def swap(message, sizes, axis, kind):
    names, pairs = partner_pairs(sizes, axis, kind)
    return lax.ppermute(message, names, pairs)


def kinds_of(n):
    return ("A", "B") if n > 2 else ("A",) if n > 1 else ()


def extend(cells, sizes, axis, dim):
    size = cells.shape[dim]
    parts = [cells]
    for kind in kinds_of(sizes[axis]):
        at = size - 1 if kind == "A" else 0
        parts.append(swap(lax.slice_in_dim(cells, at, at + 1, axis=dim), sizes, axis, kind))
    return jnp.concatenate(parts, axis=dim)


def order_of(size, n):
    return list(range(1, size + 1)) + [{"A": size + 1, "B": 0}[k] for k in kinds_of(n)]


class Plan:
    def __init__(self, sizes, extents, slots):
        self.sizes, self.extents, self.slots = sizes, extents, slots
        self.lx, self.ly, self.lz = extents
        self.X = order_of(self.lx, sizes["gx"])
        self.Y = order_of(self.ly, sizes["gy"])
        self.columns = len(self.X) * len(self.Y)
        self.cells = self.columns * self.lz
        self.own_columns = [(x, y) for x in range(1, self.lx + 1) for y in range(1, self.ly + 1)]
        self.own_cells = [(x, y, z) for x, y in self.own_columns for z in range(1, self.lz + 1)]
        self.owns = len(self.own_cells)

    def column_index(self, x, y):
        return self.X.index(x) * len(self.Y) + self.Y.index(y)

    def cell_index(self, x, y, z):
        return self.column_index(x, y) * self.lz + z - 1

    def near_columns(self, x, y):
        return [
            self.column_index(x + a, y + b)
            for a in (-1, 0, 1)
            for b in (-1, 0, 1)
            if x + a in self.X and y + b in self.Y
        ]

    def near_cells(self, x, y, z):
        return [k * self.lz + c - 1 for k in self.near_columns(x, y) for c in (z - 1, z, z + 1) if 1 <= c <= self.lz]

    def beside(self, side):
        z = self.lz if side == 0 else 1
        return [(o, cell) for o, cell in enumerate(self.own_cells) if cell[2] == z]

    def lanes(self, cell):
        return self.own_columns.index(cell[:2]), pl.ds((cell[2] - 1) * self.slots, self.slots)


GROUPS_J = (0, 0, 1, 1, 0, 2)
GROUPS_I = (0, 1, 0, 1, 2, 0)
DEPTH = 32
ROWS = 16
BF16 = jnp.bfloat16
F32 = jnp.float32


def split3(x):
    high = x.astype(BF16).astype(F32)
    rest = x - high
    middle = rest.astype(BF16).astype(F32)
    return high, middle, rest - middle


def dot(a, b):
    return jnp.dot(a, b, preferred_element_type=F32)


def groups_of(rows):
    return [(a, min(SUB, rows - a)) for a in range(0, rows, SUB)]


def put_features(out, values, order, first, count):
    parts = [split3(v) for v in values]
    for group, which in enumerate(order):
        for r, part in enumerate(parts):
            out[pl.ds(first * DEPTH + group * len(values) + r, count, stride=DEPTH), :] = part[which]
    zero = jnp.zeros_like(values[0])
    for r in range(len(order) * len(values), DEPTH):
        out[pl.ds(first * DEPTH + r, count, stride=DEPTH), :] = zero


def near_features(x, y, z, g):
    return [g * (1.0 - (x * x + y * y + z * z)), -g, 2.0 * g * x, 2.0 * g * y, 2.0 * g * z]


AXES = ("gx", "gy", "gz")


class Places:
    def __init__(self, plan):
        self.mirrored, self.shift, self.inside = [], [], []
        for k, axis in enumerate(AXES):
            extent, n = plan.extents[k], plan.sizes[axis]
            i = lax.axis_index(axis)
            odd = lax.rem(i, 2) == 1
            self.mirrored.append(odd)
            sign = jnp.where(odd, -1.0, 1.0).astype(F32)
            self.shift.append([sign * (p - 0.5 * (extent + 1)) - 0.5 for p in range(extent + 2)])
            above = jnp.where(jnp.where(odd, i - 1, i + 1) < n, 1.0, 0.0).astype(F32)
            below = jnp.where(odd, jnp.where(i + 1 < n, 1.0, 0.0), jnp.where(i > 0, 1.0, 0.0)).astype(F32)
            self.inside.append([below] + [jnp.float32(1.0)] * extent + [above])

    def source_position(self, plan, cell):
        return [jnp.where(self.mirrored[k], plan.extents[k] - cell[k], cell[k] - 1) for k in range(3)]

    def source(self, plan, cell):
        x, y, z = self.source_position(plan, cell)
        return (x * plan.extents[1] + y) * plan.extents[2] + z


def pattern(values, period, slots):
    at = lax.broadcasted_iota(jnp.int32, (len(values) * period, slots), 0)
    out = jnp.full(at.shape, values[0])
    for r in range(1, len(values)):
        out = jnp.where(at >= r * period, values[r], out)
    return out


def place_cells(plan, places, ref, out, xs, ys, zs):
    slots, rows = plan.slots, len(ys) * len(zs)
    cells = rows * len(xs)
    shift_y = pattern([places.shift[1][y] for y in ys], len(zs), slots)
    keep_y = pattern([places.inside[1][y] for y in ys], len(zs), slots)
    if len(zs) == 1:
        shift_z, keep_z = places.shift[2][zs[0]], places.inside[2][zs[0]]
    else:
        at = lax.rem(lax.broadcasted_iota(jnp.int32, (rows, slots), 0), len(zs))
        shift_z, keep_z = jnp.full(at.shape, places.shift[2][zs[0]]), 1.0
        for r in range(1, len(zs)):
            shift_z = jnp.where(at == r, places.shift[2][zs[r]], shift_z)
    keep_yz = keep_y * keep_z
    for g, x in enumerate(xs):
        at = [pl.ds(f * cells + g * rows, rows) for f in range(4)]
        out[at[0], :] = ref[at[0], :] + places.shift[0][x]
        out[at[1], :] = ref[at[1], :] + shift_y
        out[at[2], :] = ref[at[2], :] + shift_z
        out[at[3], :] = ref[at[3], :] * (keep_yz * places.inside[0][x])


def own_range(plan, k):
    return list(range(1, plan.extents[k] + 1))


def numbers_of(state, plan):
    full = jnp.where(state[pl.ds(3 * plan.owns, plan.owns), :] > 0.0, 1.0, 0.0)
    return [jnp.sum(full[o : o + 1, :]).astype(jnp.int32) for o in range(plan.owns)]


def near_operand(staged, left, ref, cells, first):
    slots = ref.shape[1]
    for start, count in groups_of(cells):
        values = near_features(*(ref[pl.ds(f * cells + start, count), :] for f in range(4)))
        put_features(staged, values, GROUPS_J, first + start, count)
    for c in range(first, first + cells):
        left[pl.ds(c * slots, slots), :] = staged[pl.ds(c * DEPTH, DEPTH), :].T.astype(BF16)


def prepare_kernel(plan, *refs):
    state, speed = refs[4], refs[5]
    fetched, sems = refs[6:10], refs[10]
    copies = [pltpu.make_async_copy(a, b, sems.at[i]) for i, (a, b) in enumerate(zip(refs[:4], fetched))]
    for copy in copies:
        copy.start()
    owns, slots = plan.owns, plan.slots
    places = Places(plan)
    for copy in copies:
        copy.wait()
    counts, mass, offsets, velocity = fetched
    row = lax.broadcasted_iota(jnp.int32, plan.extents[1:], 0)
    column = lax.broadcasted_iota(jnp.int32, plan.extents[1:], 1)
    line = lax.broadcasted_iota(jnp.int32, (owns, slots), 0)
    held = jnp.zeros((owns, slots), F32)
    for o, cell in enumerate(plan.own_cells):
        at = places.source(plan, cell)
        x, y, z = places.source_position(plan, cell)
        number = jnp.sum(jnp.where((row == y) & (column == z), counts[x].astype(F32), 0.0))
        held = jnp.where(line == o, number, held)
        for f in range(3):
            state[pl.ds(f * owns + o, 1), :] = offsets[pl.ds(f * owns + at, 1), :]
        state[pl.ds(3 * owns + o, 1), :] = mass[pl.ds(at, 1), :]
    heavy = state[pl.ds(3 * owns, owns), :] * KERNEL_NORM
    root = jnp.exp(jnp.log(heavy) * (1.0 / 3.0))
    root = root * (2.0 / 3.0) + heavy / (3.0 * root * root)
    lane = lax.broadcasted_iota(jnp.int32, (owns, slots), 1).astype(F32)
    state[pl.ds(3 * owns, owns), :] = jnp.where(lane < held, root, 0.0)
    for o, cell in enumerate(plan.own_cells):
        at = places.source(plan, cell)
        for f in range(3):
            speed[pl.ds(f * owns + o, 1), :] = velocity[pl.ds(f * owns + at, 1), :] * (1.0 / 6.0)


def cubes(left, right):
    q = jnp.maximum(dot(left, right), 0.0)
    return jnp.sum((q * q * q).reshape(q.shape[0] // SUB, SUB, q.shape[1]), axis=0)


def density_block_kernel(plan, raw, cells, right, sums, staged, own, left):
    slots = plan.slots
    place_cells(plan, Places(plan), raw, cells, plan.X, plan.Y, own_range(plan, 2))
    near_operand(staged, left, cells, plan.cells, 0)
    for p, (x, y) in enumerate(plan.own_columns):
        for z in range(plan.lz):
            c = plan.cell_index(x, y, z + 1)
            line = [cells[pl.ds(f * plan.cells + c, 1), :] for f in range(3)]
            values = [jnp.ones_like(line[0]), line[0] * line[0] + line[1] * line[1] + line[2] * line[2], *line]
            put_features(own, values, GROUPS_I, 0, 1)
            right[p, :, pl.ds(z * slots, slots)] = own[...].astype(BF16)
    for p, (x, y) in enumerate(plan.own_columns):
        mine = right[p]
        total = jnp.zeros((SUB, plan.lz * slots), F32)
        for k in plan.near_columns(x, y):
            total += cubes(left[pl.ds(k * plan.lz * slots, plan.lz * slots), :], mine)
        sums[p] = total


def density_side(plan, side, raw, placed, right, sums, staged, left):
    slots = plan.slots
    places = Places(plan)
    place_cells(plan, places, raw, placed, plan.X, plan.Y, [plan.lz + 1 if side == 0 else 0])
    near_operand(staged, left, placed, plan.columns, 0)
    out = {}
    for o, cell in plan.beside(side):
        p, lanes = plan.lanes(cell)
        total = sums[p, :, lanes]
        mine = right[p, :, lanes]
        for k in plan.near_columns(*cell[:2]):
            total += cubes(left[pl.ds(k * slots, slots), :], mine)
        out[o] = total
    return out


def density_above_kernel(plan, raw, right, sums, placed, out, staged, left):
    done = density_side(plan, 0, raw, placed, right, sums, staged, left)
    for o, cell in enumerate(plan.own_cells):
        p, lanes = plan.lanes(cell)
        out[p, :, lanes] = done[o] if o in done else sums[p, :, lanes]


def density_below_kernel(plan, raw, state, speed, right, sums, placed, flow, density, staged, left):
    owns = plan.owns
    done = density_side(plan, 1, raw, placed, right, sums, staged, left)
    rows = []
    for o, cell in enumerate(plan.own_cells):
        p, lanes = plan.lanes(cell)
        rows.append(jnp.sum(done[o] if o in done else sums[p, :, lanes], axis=0, keepdims=True))
    total = jnp.concatenate(rows, axis=0)
    full = state[pl.ds(3 * owns, owns), :] > 0.0
    flow[pl.ds(0, 3 * owns), :] = speed[...]
    flow[pl.ds(3 * owns, owns), :] = PRESSURE_COEF / jnp.where(full, total, 1.0)
    density[...] = jnp.where(full, total, 0.0)


def gather_fields(out, near, flow, cells):
    for start, count in groups_of(cells):
        rows = [pl.ds(f * cells + start, count) for f in range(8)]
        g = near[rows[3], :]
        m = g * g * g
        for f in range(3):
            out[rows[f], :] = near[rows[f], :]
            out[rows[5 + f], :] = flow[rows[f], :]
        out[rows[3], :] = m
        out[rows[4], :] = m * flow[rows[3], :]


def pack(plan, fields, cells, chosen, counts, out):
    slots = plan.slots
    lane = lax.broadcasted_iota(jnp.int32, (SUB, slots), 1)
    size = jnp.int32(0)
    for c in chosen:
        edge = lax.rem(size, slots)
        block = lax.div(size, slots)
        moved = pltpu.roll(fields[pl.ds(c, SUB, stride=cells), :], edge, 1)
        out[block] = jnp.where(lane < edge, out[block], moved)
        out[block + 1] = jnp.where(lane < edge, moved, 0.0)
        size += counts[c]
    return lax.div(size + (slots - 1), slots)


def counts_of(fields, cells, chosen):
    return {c: jnp.sum(jnp.where(fields[pl.ds(3 * cells + c, 1), :] > 0.0, 1.0, 0.0)).astype(jnp.int32) for c in chosen}


def force_pairs(packed, blocks, limit, numbers, first, last, columns, press, sums, add):
    def with_blocks(used):
        def cell(o, carry):
            def step(i, inner):
                base = pl.multiple_of(i * ROWS, ROWS)
                at = [pl.ds(base + r, SUB) for r in range(0, ROWS, SUB)]
                own = [[*(columns[f, o, a, :] for f in range(3)), press[o, a, :]] for a in at]
                total = [[sums[k, o, a, :] for k in range(4)] if add else [None] * 4 for a in at]
                plus = lambda old, new: new if old is None else old + new
                for b in range(used):
                    x, y, z, m, c, *v = (packed[b, pl.ds(f, SUB, stride=0), :] for f in range(8))
                    for r in range(len(at)):
                        d = [own[r][0] - x, own[r][1] - y, own[r][2] - z]
                        q = jnp.maximum(1.0 - (d[0] * d[0] + d[1] * d[1] + d[2] * d[2]), 0.0)
                        q2 = q * q
                        p = (m * own[r][3] + c) * q2
                        w = c * (q2 * q)
                        total[r][3] = plus(total[r][3], w)
                        for f in range(3):
                            total[r][f] = plus(total[r][f], p * d[f] + w * v[f])
                for r, a in enumerate(at):
                    for k in range(4):
                        sums[k, o, a, :] = total[r][k]
                return inner

            lax.fori_loop(0, lax.div(numbers[o] + (ROWS - 1), ROWS), step, 0)
            return carry

        if last - first == 1:
            cell(first, 0)
        else:
            lax.fori_loop(first, last, cell, 0)

    for used in range(1, limit + 1):
        pl.when(blocks == used)(functools.partial(with_blocks, used))


def repeat(rows, out, slots):
    count = rows.shape[0]
    table = jnp.concatenate([rows, jnp.zeros((slots - count, slots), F32)], axis=0).T
    for e in range(count):
        out[e] = jnp.broadcast_to(table[:, e : e + 1], (slots, slots))


def repeat_places_kernel(plan, state, out, placed):
    place_cells(plan, Places(plan), state, placed, *(own_range(plan, k) for k in range(3)))
    for f in range(3):
        repeat(placed[pl.ds(f * plan.owns, plan.owns), :], out.at[f], plan.slots)


def repeat_press_kernel(plan, flow, density, out, ordered):
    places = Places(plan)
    for o, cell in enumerate(plan.own_cells):
        ordered[pl.ds(places.source(plan, cell), 1), :] = density[pl.ds(o, 1), :]
    repeat(flow[pl.ds(3 * plan.owns, plan.owns), :], out, plan.slots)


def note_numbers(plan, state, numbers):
    for o, number in enumerate(numbers_of(state, plan)):
        numbers[o] = number


def force_own_kernel(plan, cells, flow, columns, press, sums, fields, placed, packed, numbers):
    owns = plan.owns
    note_numbers(plan, cells, numbers)
    place_cells(plan, Places(plan), cells, placed, *(own_range(plan, k) for k in range(3)))
    gather_fields(fields, placed, flow, owns)
    chosen = list(range(owns))
    used = pack(plan, fields, owns, chosen, [numbers[o] for o in chosen], packed)
    force_pairs(packed, used, owns, numbers, 0, owns, columns, press, sums, False)


def force_block_kernel(plan, state, cells, flow, columns, press, start, sums, fields, packed, numbers):
    note_numbers(plan, state, numbers)
    gather_fields(fields, cells, flow, plan.cells)
    mine = [plan.column_index(x, y) for x, y in plan.own_columns]
    near = [
        [k * plan.lz + z for k in plan.near_columns(x, y) if k not in mine for z in range(plan.lz)]
        for x, y in plan.own_columns
    ]
    counts = counts_of(fields, plan.cells, sorted(set(sum(near, []))))
    used = [pack(plan, fields, plan.cells, chosen, counts, packed.at[p]) for p, chosen in enumerate(near)]
    for p, chosen in enumerate(near):
        first = p * plan.lz
        force_pairs(packed.at[p], used[p], len(chosen), numbers, first, first + plan.lz, columns, press, sums, True)


def force_side(plan, side, state, near, flow, columns, press, sums, fields, packed, numbers):
    n = plan.columns
    note_numbers(plan, state, numbers)
    gather_fields(fields, near, flow, n)
    counts = counts_of(fields, n, range(n))
    lists = [(o, plan.near_columns(*cell[:2])) for o, cell in plan.beside(side)]
    used = [pack(plan, fields, n, chosen, counts, packed.at[p]) for p, (_, chosen) in enumerate(lists)]
    for p, (o, chosen) in enumerate(lists):
        force_pairs(packed.at[p], used[p], len(chosen), numbers, o, o + 1, columns, press, sums, True)


def totals(plan, chosen, table):
    lane = lax.broadcasted_iota(jnp.int32, table.shape, 1)
    for o, sums in chosen:
        for k in range(4):
            table = jnp.where(lane == k * plan.owns + o, jnp.sum(sums[k, o], axis=1, keepdims=True), table)
    return table


def force_above_kernel(plan, state, near, flow, columns, press, start, sums, table, *scratch):
    force_side(plan, 0, state, near, flow, columns, press, sums, *scratch)
    mine = [] if plan.lz == 1 else [(o, sums) for o, _ in plan.beside(0)]
    table[...] = totals(plan, mine, jnp.zeros(table.shape, F32))


def force_below_kernel(plan, state, own, near, flow, columns, press, start, above, sums, accel, *scratch):
    owns = plan.owns
    force_side(plan, 1, state, near, flow, columns, press, sums, *scratch)
    known = [] if plan.lz == 1 else [o for o, _ in plan.beside(0)]
    mine = [(o, sums) for o in range(owns) if o not in known]
    whole = totals(plan, mine, above[...]).T
    places = Places(plan)
    full = state[pl.ds(3 * owns, owns), :] > 0.0
    for f in range(3):
        v = own[pl.ds(f * owns, owns), :]
        value = 6.0 * (whole[f * owns : (f + 1) * owns] - v * whole[3 * owns : 4 * owns])
        value = jnp.where(full, value, 0.0)
        for o, cell in enumerate(plan.own_cells):
            accel[pl.ds(f * owns + places.source(plan, cell), 1), :] = value[o : o + 1, :]


def call(kernel, args, outs, scratch, cost, aliases=None, place=pltpu.VMEM):
    vmem = pl.BlockSpec(memory_space=pltpu.VMEM)
    return pl.pallas_call(
        kernel,
        out_shape=[jax.ShapeDtypeStruct(shape, dtype) for shape, dtype in outs],
        in_specs=[pl.BlockSpec(memory_space=place)] * len(args),
        out_specs=[vmem] * len(outs),
        scratch_shapes=scratch,
        input_output_aliases=aliases or {},
        cost_estimate=pl.CostEstimate(flops=cost, bytes_accessed=1 << 20, transcendentals=0),
        compiler_params=pltpu.CompilerParams(vmem_limit_bytes=16 << 20),
    )(*args)


def local(sizes, offsets, velocity, mass, counts):
    slots = offsets.shape[-1]
    extents = offsets.shape[1:4]
    plan = Plan(sizes, extents, slots)
    pairs, lz, total, columns, owns = len(plan.own_columns), plan.lz, plan.cells, plan.columns, plan.owns
    flat = lambda cells: cells.reshape(-1, slots)

    def gather(state):
        block = extend(state.reshape((4,) + extents + (slots,)), sizes, "gx", 1)
        block = extend(block, sizes, "gy", 2)
        sides = []
        for kind in ("A", "B"):
            at = lz - 1 if kind == "A" else 0
            message = lax.slice_in_dim(block, at, at + 1, axis=3)
            present = kind in kinds_of(sizes["gz"])
            sides.append(flat(swap(message, sizes, "gz", kind) if present else jnp.zeros_like(message)))
        return flat(block), sides

    stay = lambda x: pltpu.with_memory_space_constraint(x, pltpu.HBM)
    state, speed = call(
        functools.partial(prepare_kernel, plan),
        [stay(counts), stay(flat(mass)), stay(flat(offsets)), stay(flat(velocity))],
        [((4 * owns, slots), F32), ((3 * owns, slots), F32)],
        [
            pltpu.VMEM(tuple(extents), jnp.int32),
            pltpu.VMEM((owns, slots), F32),
            pltpu.VMEM((3 * owns, slots), F32),
            pltpu.VMEM((3 * owns, slots), F32),
            pltpu.SemaphoreType.DMA((4,)),
        ],
        1 << 20,
        place=pltpu.HBM,
    )
    wide = (owns, slots, slots)
    (places,) = call(
        functools.partial(repeat_places_kernel, plan),
        [state],
        [((3,) + wide, F32)],
        [pltpu.VMEM((4 * owns, slots), F32)],
        1 << 26,
    )
    raw, (raw_a, raw_b) = gather(state)
    cells, right, sums = call(
        functools.partial(density_block_kernel, plan),
        [raw],
        [
            ((4 * total, slots), F32),
            ((pairs, DEPTH, lz * slots), BF16),
            ((pairs, SUB, lz * slots), F32),
        ],
        [
            pltpu.VMEM((total * DEPTH, slots), F32),
            pltpu.VMEM((DEPTH, slots), F32),
            pltpu.VMEM((total * slots, DEPTH), BF16),
        ],
        1 << 27,
    )
    side = ((4 * columns, slots), F32)
    side_scratch = [pltpu.VMEM((columns * DEPTH, slots), F32), pltpu.VMEM((columns * slots, DEPTH), BF16)]
    za, sums = call(
        functools.partial(density_above_kernel, plan),
        [raw_a, right, sums],
        [side, ((pairs, SUB, lz * slots), F32)],
        side_scratch,
        1 << 25,
    )
    zb, flow_state, density = call(
        functools.partial(density_below_kernel, plan),
        [raw_b, state, speed, right, sums],
        [side, ((4 * owns, slots), F32), ((owns, slots), F32)],
        side_scratch,
        1 << 25,
    )
    flow, (fza, fzb) = gather(flow_state)
    press, density = call(
        functools.partial(repeat_press_kernel, plan),
        [flow_state, density],
        [(wide, F32), ((owns, slots), F32)],
        [],
        1 << 25,
    )
    four = ((4,) + wide, F32)
    numbers = pltpu.SMEM((owns,), jnp.int32)

    def scratch_of(cells, lists, most):
        return [pltpu.VMEM((8 * cells, slots), F32), pltpu.VMEM((*lists, most + 2, SUB, slots), F32), numbers]

    most = max(len(plan.near_columns(*cell[:2])) for cell in plan.own_cells)
    fields, packed, _ = scratch_of(owns, (), owns)
    (partial,) = call(
        functools.partial(force_own_kernel, plan),
        [state, flow_state, places, press],
        [four],
        [fields, pltpu.VMEM((4 * owns, slots), F32), packed, numbers],
        1 << 27,
    )
    (partial,) = call(
        functools.partial(force_block_kernel, plan),
        [state, cells, flow, places, press, partial],
        [four],
        scratch_of(total, (pairs,), most * lz),
        1 << 27,
        {5: 0},
    )
    partial, table = call(
        functools.partial(force_above_kernel, plan),
        [state, za, fza, places, press, partial],
        [four, ((slots, slots), F32)],
        scratch_of(columns, (pairs,), most),
        1 << 26,
        {5: 0},
    )
    _, force = call(
        functools.partial(force_below_kernel, plan),
        [state, flow_state, zb, fzb, places, press, partial, table],
        [four, ((3 * owns, slots), F32)],
        scratch_of(columns, (pairs,), most),
        1 << 26,
        {6: 0},
    )
    return force.reshape(offsets.shape), density.reshape(mass.shape)


def layer(sizes, *args):
    return local(sizes, *args)


def solution(mesh):
    sizes = dict(mesh.shape)
    in_specs = (
        P(None, "gx", "gy", "gz", None),
        P(None, "gx", "gy", "gz", None),
        P("gx", "gy", "gz", None),
        P("gx", "gy", "gz"),
    )
    out_specs = (P(None, "gx", "gy", "gz", None), P("gx", "gy", "gz", None))
    step = jax.shard_map(
        functools.partial(layer, sizes), mesh=mesh, in_specs=in_specs, out_specs=out_specs, check_vma=False
    )
    if min(sizes[a] for a in AXES) < 2:
        return step
    return step
```

```python
import functools
import math

import jax
import jax.numpy as jnp
from jax import lax
from jax.experimental import pallas as pl
from jax.experimental.pallas import tpu as pltpu
from jax.sharding import PartitionSpec as P

KERNEL_NORM = 315.0 / (64.0 * math.pi)
PRESSURE_COEF = 0.5
SUB = 8


def partner_pairs(sizes, axis, kind):
    n, nx = sizes[axis], sizes["gx"]
    pairs = []
    for i in range(n):
        j = (i ^ 1) if kind == "A" else ((i - 1) ^ 1) + 1
        if i == 0 and kind == "B" or j >= n or j < 0:
            j = i
        pairs.append(j)
    if axis == "gx":
        if kind == "B":
            pairs[0], pairs[n - 1] = n - 1, 0
        return "gx", [(i, j) for i, j in enumerate(pairs)]
    if all(i != j for i, j in enumerate(pairs)):
        return axis, list(enumerate(pairs))
    out = []
    for x in range(nx):
        for i, j in enumerate(pairs):
            to = (x, j)
            if i == j and nx % 2 == 0:
                to = (x ^ 1, j)
            out.append((x * n + i, to[0] * n + to[1]))
    return ("gx", axis), out


def swap(message, sizes, axis, kind):
    names, pairs = partner_pairs(sizes, axis, kind)
    return lax.ppermute(message, names, pairs)


def kinds_of(n):
    return ("A", "B") if n > 2 else ("A",) if n > 1 else ()


def extend(cells, sizes, axis, dim):
    size = cells.shape[dim]
    parts = [cells]
    for kind in kinds_of(sizes[axis]):
        at = size - 1 if kind == "A" else 0
        parts.append(swap(lax.slice_in_dim(cells, at, at + 1, axis=dim), sizes, axis, kind))
    return jnp.concatenate(parts, axis=dim)


def order_of(size, n):
    return list(range(1, size + 1)) + [{"A": size + 1, "B": 0}[k] for k in kinds_of(n)]


class Plan:
    def __init__(self, sizes, extents, slots):
        self.sizes, self.extents, self.slots = sizes, extents, slots
        self.lx, self.ly, self.lz = extents
        self.X = order_of(self.lx, sizes["gx"])
        self.Y = order_of(self.ly, sizes["gy"])
        self.columns = len(self.X) * len(self.Y)
        self.cells = self.columns * self.lz
        self.own_columns = [(x, y) for x in range(1, self.lx + 1) for y in range(1, self.ly + 1)]
        self.own_cells = [(x, y, z) for x, y in self.own_columns for z in range(1, self.lz + 1)]
        self.owns = len(self.own_cells)

    def column_index(self, x, y):
        return self.X.index(x) * len(self.Y) + self.Y.index(y)

    def cell_index(self, x, y, z):
        return self.column_index(x, y) * self.lz + z - 1

    def near_columns(self, x, y):
        return [
            self.column_index(x + a, y + b)
            for a in (-1, 0, 1)
            for b in (-1, 0, 1)
            if x + a in self.X and y + b in self.Y
        ]

    def near_cells(self, x, y, z):
        return [k * self.lz + c - 1 for k in self.near_columns(x, y) for c in (z - 1, z, z + 1) if 1 <= c <= self.lz]

    def beside(self, side):
        z = self.lz if side == 0 else 1
        return [(o, cell) for o, cell in enumerate(self.own_cells) if cell[2] == z]

    def lanes(self, cell):
        return self.own_columns.index(cell[:2]), pl.ds((cell[2] - 1) * self.slots, self.slots)


GROUPS_J = (0, 0, 1, 1, 0, 2)
GROUPS_I = (0, 1, 0, 1, 2, 0)
DEPTH = 32
ROWS = 16
BF16 = jnp.bfloat16
F32 = jnp.float32


def split3(x):
    high = x.astype(BF16).astype(F32)
    rest = x - high
    middle = rest.astype(BF16).astype(F32)
    return high, middle, rest - middle


def dot(a, b):
    return jnp.dot(a, b, preferred_element_type=F32)


def groups_of(rows):
    return [(a, min(SUB, rows - a)) for a in range(0, rows, SUB)]


def put_features(out, values, order, first, count):
    parts = [split3(v) for v in values]
    for group, which in enumerate(order):
        for r, part in enumerate(parts):
            out[pl.ds(first * DEPTH + group * len(values) + r, count, stride=DEPTH), :] = part[which]
    zero = jnp.zeros_like(values[0])
    for r in range(len(order) * len(values), DEPTH):
        out[pl.ds(first * DEPTH + r, count, stride=DEPTH), :] = zero


def near_features(x, y, z, g):
    return [g * (1.0 - (x * x + y * y + z * z)), -g, 2.0 * g * x, 2.0 * g * y, 2.0 * g * z]


AXES = ("gx", "gy", "gz")


class Places:
    def __init__(self, plan):
        self.mirrored, self.shift, self.inside = [], [], []
        for k, axis in enumerate(AXES):
            extent, n = plan.extents[k], plan.sizes[axis]
            i = lax.axis_index(axis)
            odd = lax.rem(i, 2) == 1
            self.mirrored.append(odd)
            sign = jnp.where(odd, -1.0, 1.0).astype(F32)
            self.shift.append([sign * (p - 0.5 * (extent + 1)) - 0.5 for p in range(extent + 2)])
            above = jnp.where(jnp.where(odd, i - 1, i + 1) < n, 1.0, 0.0).astype(F32)
            below = jnp.where(odd, jnp.where(i + 1 < n, 1.0, 0.0), jnp.where(i > 0, 1.0, 0.0)).astype(F32)
            self.inside.append([below] + [jnp.float32(1.0)] * extent + [above])

    def source_position(self, plan, cell):
        return [jnp.where(self.mirrored[k], plan.extents[k] - cell[k], cell[k] - 1) for k in range(3)]

    def source(self, plan, cell):
        x, y, z = self.source_position(plan, cell)
        return (x * plan.extents[1] + y) * plan.extents[2] + z


def pattern(values, period, slots):
    at = lax.broadcasted_iota(jnp.int32, (len(values) * period, slots), 0)
    out = jnp.full(at.shape, values[0])
    for r in range(1, len(values)):
        out = jnp.where(at >= r * period, values[r], out)
    return out


def place_cells(plan, places, ref, out, xs, ys, zs):
    slots, rows = plan.slots, len(ys) * len(zs)
    cells = rows * len(xs)
    shift_y = pattern([places.shift[1][y] for y in ys], len(zs), slots)
    keep_y = pattern([places.inside[1][y] for y in ys], len(zs), slots)
    if len(zs) == 1:
        shift_z, keep_z = places.shift[2][zs[0]], places.inside[2][zs[0]]
    else:
        at = lax.rem(lax.broadcasted_iota(jnp.int32, (rows, slots), 0), len(zs))
        shift_z, keep_z = jnp.full(at.shape, places.shift[2][zs[0]]), 1.0
        for r in range(1, len(zs)):
            shift_z = jnp.where(at == r, places.shift[2][zs[r]], shift_z)
    keep_yz = keep_y * keep_z
    for g, x in enumerate(xs):
        at = [pl.ds(f * cells + g * rows, rows) for f in range(4)]
        out[at[0], :] = ref[at[0], :] + places.shift[0][x]
        out[at[1], :] = ref[at[1], :] + shift_y
        out[at[2], :] = ref[at[2], :] + shift_z
        out[at[3], :] = ref[at[3], :] * (keep_yz * places.inside[0][x])


def own_range(plan, k):
    return list(range(1, plan.extents[k] + 1))


def numbers_of(state, plan):
    full = jnp.where(state[pl.ds(3 * plan.owns, plan.owns), :] > 0.0, 1.0, 0.0)
    return [jnp.sum(full[o : o + 1, :]).astype(jnp.int32) for o in range(plan.owns)]


def near_operand(staged, left, ref, cells, first):
    slots = ref.shape[1]
    for start, count in groups_of(cells):
        values = near_features(*(ref[pl.ds(f * cells + start, count), :] for f in range(4)))
        put_features(staged, values, GROUPS_J, first + start, count)
    for c in range(first, first + cells):
        left[pl.ds(c * slots, slots), :] = staged[pl.ds(c * DEPTH, DEPTH), :].T.astype(BF16)


def prepare_kernel(plan, *refs):
    state, speed = refs[4], refs[5]
    fetched, sems = refs[6:10], refs[10]
    copies = [pltpu.make_async_copy(a, b, sems.at[i]) for i, (a, b) in enumerate(zip(refs[:4], fetched))]
    for copy in copies:
        copy.start()
    owns, slots = plan.owns, plan.slots
    places = Places(plan)
    for copy in copies:
        copy.wait()
    counts, mass, offsets, velocity = fetched
    row = lax.broadcasted_iota(jnp.int32, plan.extents[1:], 0)
    column = lax.broadcasted_iota(jnp.int32, plan.extents[1:], 1)
    line = lax.broadcasted_iota(jnp.int32, (owns, slots), 0)
    held = jnp.zeros((owns, slots), F32)
    for o, cell in enumerate(plan.own_cells):
        at = places.source(plan, cell)
        x, y, z = places.source_position(plan, cell)
        number = jnp.sum(jnp.where((row == y) & (column == z), counts[x].astype(F32), 0.0))
        held = jnp.where(line == o, number, held)
        for f in range(3):
            state[pl.ds(f * owns + o, 1), :] = offsets[pl.ds(f * owns + at, 1), :]
        state[pl.ds(3 * owns + o, 1), :] = mass[pl.ds(at, 1), :]
    heavy = state[pl.ds(3 * owns, owns), :] * KERNEL_NORM
    root = jnp.exp(jnp.log(heavy) * (1.0 / 3.0))
    root = root * (2.0 / 3.0) + heavy / (3.0 * root * root)
    lane = lax.broadcasted_iota(jnp.int32, (owns, slots), 1).astype(F32)
    state[pl.ds(3 * owns, owns), :] = jnp.where(lane < held, root, 0.0)
    for o, cell in enumerate(plan.own_cells):
        at = places.source(plan, cell)
        for f in range(3):
            speed[pl.ds(f * owns + o, 1), :] = velocity[pl.ds(f * owns + at, 1), :] * (1.0 / 6.0)


def cubes(left, right):
    q = jnp.maximum(dot(left, right), 0.0)
    return jnp.sum((q * q * q).reshape(q.shape[0] // SUB, SUB, q.shape[1]), axis=0)


def density_block_kernel(plan, raw, cells, right, sums, staged, own, left):
    slots = plan.slots
    place_cells(plan, Places(plan), raw, cells, plan.X, plan.Y, own_range(plan, 2))
    near_operand(staged, left, cells, plan.cells, 0)
    for p, (x, y) in enumerate(plan.own_columns):
        for z in range(plan.lz):
            c = plan.cell_index(x, y, z + 1)
            line = [cells[pl.ds(f * plan.cells + c, 1), :] for f in range(3)]
            values = [jnp.ones_like(line[0]), line[0] * line[0] + line[1] * line[1] + line[2] * line[2], *line]
            put_features(own, values, GROUPS_I, 0, 1)
            right[p, :, pl.ds(z * slots, slots)] = own[...].astype(BF16)
    for p, (x, y) in enumerate(plan.own_columns):
        mine = right[p]
        total = jnp.zeros((SUB, plan.lz * slots), F32)
        for k in plan.near_columns(x, y):
            total += cubes(left[pl.ds(k * plan.lz * slots, plan.lz * slots), :], mine)
        sums[p] = total


def density_side(plan, side, raw, placed, right, sums, staged, left):
    slots = plan.slots
    places = Places(plan)
    place_cells(plan, places, raw, placed, plan.X, plan.Y, [plan.lz + 1 if side == 0 else 0])
    near_operand(staged, left, placed, plan.columns, 0)
    out = {}
    for o, cell in plan.beside(side):
        p, lanes = plan.lanes(cell)
        total = sums[p, :, lanes]
        mine = right[p, :, lanes]
        for k in plan.near_columns(*cell[:2]):
            total += cubes(left[pl.ds(k * slots, slots), :], mine)
        out[o] = total
    return out


def density_above_kernel(plan, raw, right, sums, placed, out, staged, left):
    done = density_side(plan, 0, raw, placed, right, sums, staged, left)
    for o, cell in enumerate(plan.own_cells):
        p, lanes = plan.lanes(cell)
        out[p, :, lanes] = done[o] if o in done else sums[p, :, lanes]


def density_below_kernel(plan, raw, state, speed, right, sums, placed, flow, density, staged, left):
    owns = plan.owns
    done = density_side(plan, 1, raw, placed, right, sums, staged, left)
    rows = []
    for o, cell in enumerate(plan.own_cells):
        p, lanes = plan.lanes(cell)
        rows.append(jnp.sum(done[o] if o in done else sums[p, :, lanes], axis=0, keepdims=True))
    total = jnp.concatenate(rows, axis=0)
    full = state[pl.ds(3 * owns, owns), :] > 0.0
    flow[pl.ds(0, 3 * owns), :] = speed[...]
    flow[pl.ds(3 * owns, owns), :] = PRESSURE_COEF / jnp.where(full, total, 1.0)
    density[...] = jnp.where(full, total, 0.0)


def gather_fields(out, near, flow, cells):
    for start, count in groups_of(cells):
        rows = [pl.ds(f * cells + start, count) for f in range(8)]
        g = near[rows[3], :]
        m = g * g * g
        for f in range(3):
            out[rows[f], :] = near[rows[f], :]
            out[rows[5 + f], :] = flow[rows[f], :]
        out[rows[3], :] = m
        out[rows[4], :] = m * flow[rows[3], :]


def pack(plan, fields, cells, chosen, counts, out):
    slots = plan.slots
    lane = lax.broadcasted_iota(jnp.int32, (SUB, slots), 1)
    size = jnp.int32(0)
    for c in chosen:
        edge = lax.rem(size, slots)
        block = lax.div(size, slots)
        moved = pltpu.roll(fields[pl.ds(c, SUB, stride=cells), :], edge, 1)
        out[block] = jnp.where(lane < edge, out[block], moved)
        out[block + 1] = jnp.where(lane < edge, moved, 0.0)
        size += counts[c]
    return lax.div(size + (slots - 1), slots)


def counts_of(fields, cells, chosen):
    return {c: jnp.sum(jnp.where(fields[pl.ds(3 * cells + c, 1), :] > 0.0, 1.0, 0.0)).astype(jnp.int32) for c in chosen}


def force_pairs(packed, blocks, limit, numbers, first, last, columns, press, sums, add):
    def with_blocks(used):
        def cell(o, carry):
            def step(i, inner):
                base = pl.multiple_of(i * ROWS, ROWS)
                at = [pl.ds(base + r, SUB) for r in range(0, ROWS, SUB)]
                own = [[*(columns[f, o, a, :] for f in range(3)), press[o, a, :]] for a in at]
                total = [[sums[k, o, a, :] for k in range(4)] if add else [None] * 4 for a in at]
                plus = lambda old, new: new if old is None else old + new
                for b in range(used):
                    x, y, z, m, c, *v = (packed[b, pl.ds(f, SUB, stride=0), :] for f in range(8))
                    for r in range(len(at)):
                        d = [own[r][0] - x, own[r][1] - y, own[r][2] - z]
                        q = jnp.maximum(1.0 - (d[0] * d[0] + d[1] * d[1] + d[2] * d[2]), 0.0)
                        q2 = q * q
                        p = (m * own[r][3] + c) * q2
                        w = c * (q2 * q)
                        total[r][3] = plus(total[r][3], w)
                        for f in range(3):
                            total[r][f] = plus(total[r][f], p * d[f] + w * v[f])
                for r, a in enumerate(at):
                    for k in range(4):
                        sums[k, o, a, :] = total[r][k]
                return inner

            lax.fori_loop(0, lax.div(numbers[o] + (ROWS - 1), ROWS), step, 0)
            return carry

        if last - first == 1:
            cell(first, 0)
        else:
            lax.fori_loop(first, last, cell, 0)

    def choose(low, high):
        if low == high:
            with_blocks(low)
            return
        middle = (low + high) // 2
        pl.when(blocks <= middle)(functools.partial(choose, low, middle))
        pl.when(blocks > middle)(functools.partial(choose, middle + 1, high))

    pl.when(blocks > 0)(functools.partial(choose, 1, limit))


def repeat(rows, out, slots):
    count = rows.shape[0]
    table = jnp.concatenate([rows, jnp.zeros((slots - count, slots), F32)], axis=0).T
    for e in range(count):
        out[e] = jnp.broadcast_to(table[:, e : e + 1], (slots, slots))


def repeat_places_kernel(plan, state, out, placed):
    place_cells(plan, Places(plan), state, placed, *(own_range(plan, k) for k in range(3)))
    for f in range(3):
        repeat(placed[pl.ds(f * plan.owns, plan.owns), :], out.at[f], plan.slots)


def repeat_press_kernel(plan, flow, density, out, ordered):
    places = Places(plan)
    for o, cell in enumerate(plan.own_cells):
        ordered[pl.ds(places.source(plan, cell), 1), :] = density[pl.ds(o, 1), :]
    repeat(flow[pl.ds(3 * plan.owns, plan.owns), :], out, plan.slots)


def note_numbers(plan, state, numbers):
    for o, number in enumerate(numbers_of(state, plan)):
        numbers[o] = number


def force_own_kernel(plan, cells, flow, columns, press, sums, fields, placed, packed, numbers):
    owns = plan.owns
    note_numbers(plan, cells, numbers)
    place_cells(plan, Places(plan), cells, placed, *(own_range(plan, k) for k in range(3)))
    gather_fields(fields, placed, flow, owns)
    chosen = list(range(owns))
    used = pack(plan, fields, owns, chosen, [numbers[o] for o in chosen], packed)
    force_pairs(packed, used, owns, numbers, 0, owns, columns, press, sums, False)


def force_block_kernel(plan, state, cells, flow, columns, press, start, sums, fields, packed, numbers):
    note_numbers(plan, state, numbers)
    gather_fields(fields, cells, flow, plan.cells)
    mine = [plan.column_index(x, y) for x, y in plan.own_columns]
    near = [
        [k * plan.lz + z for k in plan.near_columns(x, y) if k not in mine for z in range(plan.lz)]
        for x, y in plan.own_columns
    ]
    counts = counts_of(fields, plan.cells, sorted(set(sum(near, []))))
    used = [pack(plan, fields, plan.cells, chosen, counts, packed.at[p]) for p, chosen in enumerate(near)]
    for p, chosen in enumerate(near):
        first = p * plan.lz
        force_pairs(packed.at[p], used[p], len(chosen), numbers, first, first + plan.lz, columns, press, sums, True)


def force_side(plan, side, state, near, flow, columns, press, sums, fields, packed, numbers):
    n = plan.columns
    note_numbers(plan, state, numbers)
    gather_fields(fields, near, flow, n)
    counts = counts_of(fields, n, range(n))
    lists = [(o, plan.near_columns(*cell[:2])) for o, cell in plan.beside(side)]
    used = [pack(plan, fields, n, chosen, counts, packed.at[p]) for p, (_, chosen) in enumerate(lists)]
    for p, (o, chosen) in enumerate(lists):
        force_pairs(packed.at[p], used[p], len(chosen), numbers, o, o + 1, columns, press, sums, True)


def totals(plan, chosen, table):
    lane = lax.broadcasted_iota(jnp.int32, table.shape, 1)
    for o, sums in chosen:
        for k in range(4):
            table = jnp.where(lane == k * plan.owns + o, jnp.sum(sums[k, o], axis=1, keepdims=True), table)
    return table


def force_above_kernel(plan, state, near, flow, columns, press, start, sums, table, *scratch):
    force_side(plan, 0, state, near, flow, columns, press, sums, *scratch)
    mine = [] if plan.lz == 1 else [(o, sums) for o, _ in plan.beside(0)]
    table[...] = totals(plan, mine, jnp.zeros(table.shape, F32))


def force_below_kernel(plan, state, own, near, flow, columns, press, start, above, sums, accel, *scratch):
    owns = plan.owns
    force_side(plan, 1, state, near, flow, columns, press, sums, *scratch)
    known = [] if plan.lz == 1 else [o for o, _ in plan.beside(0)]
    mine = [(o, sums) for o in range(owns) if o not in known]
    whole = totals(plan, mine, above[...]).T
    places = Places(plan)
    full = state[pl.ds(3 * owns, owns), :] > 0.0
    for f in range(3):
        v = own[pl.ds(f * owns, owns), :]
        value = 6.0 * (whole[f * owns : (f + 1) * owns] - v * whole[3 * owns : 4 * owns])
        value = jnp.where(full, value, 0.0)
        for o, cell in enumerate(plan.own_cells):
            accel[pl.ds(f * owns + places.source(plan, cell), 1), :] = value[o : o + 1, :]


def call(kernel, args, outs, scratch, cost, aliases=None, place=pltpu.VMEM):
    vmem = pl.BlockSpec(memory_space=pltpu.VMEM)
    return pl.pallas_call(
        kernel,
        out_shape=[jax.ShapeDtypeStruct(shape, dtype) for shape, dtype in outs],
        in_specs=[pl.BlockSpec(memory_space=place)] * len(args),
        out_specs=[vmem] * len(outs),
        scratch_shapes=scratch,
        input_output_aliases=aliases or {},
        cost_estimate=pl.CostEstimate(flops=cost, bytes_accessed=1 << 20, transcendentals=0),
        compiler_params=pltpu.CompilerParams(vmem_limit_bytes=16 << 20),
    )(*args)


def local(sizes, offsets, velocity, mass, counts):
    slots = offsets.shape[-1]
    extents = offsets.shape[1:4]
    plan = Plan(sizes, extents, slots)
    pairs, lz, total, columns, owns = len(plan.own_columns), plan.lz, plan.cells, plan.columns, plan.owns
    flat = lambda cells: cells.reshape(-1, slots)

    def gather(state):
        block = extend(state.reshape((4,) + extents + (slots,)), sizes, "gx", 1)
        block = extend(block, sizes, "gy", 2)
        sides = []
        for kind in ("A", "B"):
            at = lz - 1 if kind == "A" else 0
            message = lax.slice_in_dim(block, at, at + 1, axis=3)
            present = kind in kinds_of(sizes["gz"])
            sides.append(flat(swap(message, sizes, "gz", kind) if present else jnp.zeros_like(message)))
        return flat(block), sides

    stay = lambda x: pltpu.with_memory_space_constraint(x, pltpu.HBM)
    state, speed = call(
        functools.partial(prepare_kernel, plan),
        [stay(counts), stay(flat(mass)), stay(flat(offsets)), stay(flat(velocity))],
        [((4 * owns, slots), F32), ((3 * owns, slots), F32)],
        [
            pltpu.VMEM(tuple(extents), jnp.int32),
            pltpu.VMEM((owns, slots), F32),
            pltpu.VMEM((3 * owns, slots), F32),
            pltpu.VMEM((3 * owns, slots), F32),
            pltpu.SemaphoreType.DMA((4,)),
        ],
        1 << 20,
        place=pltpu.HBM,
    )
    wide = (owns, slots, slots)
    (places,) = call(
        functools.partial(repeat_places_kernel, plan),
        [state],
        [((3,) + wide, F32)],
        [pltpu.VMEM((4 * owns, slots), F32)],
        1 << 26,
    )
    raw, (raw_a, raw_b) = gather(state)
    cells, right, sums = call(
        functools.partial(density_block_kernel, plan),
        [raw],
        [
            ((4 * total, slots), F32),
            ((pairs, DEPTH, lz * slots), BF16),
            ((pairs, SUB, lz * slots), F32),
        ],
        [
            pltpu.VMEM((total * DEPTH, slots), F32),
            pltpu.VMEM((DEPTH, slots), F32),
            pltpu.VMEM((total * slots, DEPTH), BF16),
        ],
        1 << 27,
    )
    side = ((4 * columns, slots), F32)
    side_scratch = [pltpu.VMEM((columns * DEPTH, slots), F32), pltpu.VMEM((columns * slots, DEPTH), BF16)]
    za, sums = call(
        functools.partial(density_above_kernel, plan),
        [raw_a, right, sums],
        [side, ((pairs, SUB, lz * slots), F32)],
        side_scratch,
        1 << 25,
    )
    zb, flow_state, density = call(
        functools.partial(density_below_kernel, plan),
        [raw_b, state, speed, right, sums],
        [side, ((4 * owns, slots), F32), ((owns, slots), F32)],
        side_scratch,
        1 << 25,
    )
    flow, (fza, fzb) = gather(flow_state)
    press, density = call(
        functools.partial(repeat_press_kernel, plan),
        [flow_state, density],
        [(wide, F32), ((owns, slots), F32)],
        [],
        1 << 25,
    )
    four = ((4,) + wide, F32)
    numbers = pltpu.SMEM((owns,), jnp.int32)

    def scratch_of(cells, lists, most):
        return [pltpu.VMEM((8 * cells, slots), F32), pltpu.VMEM((*lists, most + 2, SUB, slots), F32), numbers]

    most = max(len(plan.near_columns(*cell[:2])) for cell in plan.own_cells)
    fields, packed, _ = scratch_of(owns, (), owns)
    (partial,) = call(
        functools.partial(force_own_kernel, plan),
        [state, flow_state, places, press],
        [four],
        [fields, pltpu.VMEM((4 * owns, slots), F32), packed, numbers],
        1 << 27,
    )
    (partial,) = call(
        functools.partial(force_block_kernel, plan),
        [state, cells, flow, places, press, partial],
        [four],
        scratch_of(total, (pairs,), most * lz),
        1 << 27,
        {5: 0},
    )
    partial, table = call(
        functools.partial(force_above_kernel, plan),
        [state, za, fza, places, press, partial],
        [four, ((slots, slots), F32)],
        scratch_of(columns, (pairs,), most),
        1 << 26,
        {5: 0},
    )
    _, force = call(
        functools.partial(force_below_kernel, plan),
        [state, flow_state, zb, fzb, places, press, partial, table],
        [four, ((3 * owns, slots), F32)],
        scratch_of(columns, (pairs,), most),
        1 << 26,
        {6: 0},
    )
    return force.reshape(offsets.shape), density.reshape(mass.shape)


def layer(sizes, *args):
    return local(sizes, *args)


def solution(mesh):
    sizes = dict(mesh.shape)
    in_specs = (
        P(None, "gx", "gy", "gz", None),
        P(None, "gx", "gy", "gz", None),
        P("gx", "gy", "gz", None),
        P("gx", "gy", "gz"),
    )
    out_specs = (P(None, "gx", "gy", "gz", None), P("gx", "gy", "gz", None))
    step = jax.shard_map(
        functools.partial(layer, sizes), mesh=mesh, in_specs=in_specs, out_specs=out_specs, check_vma=False
    )
    if min(sizes[a] for a in AXES) < 2:
        return step
    return step
```
